32 devices in a mesh: row: 4 (over y, x), orb: 8 (over z, core).
Axes of the slice: x: 2, y: 2, z: 4, core: 2. Of those that a mesh axis runs over, the one named last changes fastest.
Arguments:
- integrals: bfloat16 [24, 1024, 5120], P('orb', 'row'), may hold values from -6 to 6
- tile_ids: int32 [8, 40], P('row'), may hold values from 0 to 127, as said below
- coefficients: bfloat16 [1024, 16384], P('orb'), may hold values from -0.078125 to 0.078125
- metric: float32 [24, 24], replicated, may hold values from -0.0078125 to 0.0078125
Outputs:
- exchange_columns: float32 [1024, 1024], P('orb', 'row')
The draws below stay inside these ranges and needn't reach their ends.
Inputs may be any that keep to these rules, and one draw needn't show every extreme that they name: `tile_ids`: row block b covers basis functions b * 128 to b * 128 + 127. Each row lists 40 different column tiles (tile t covers basis functions t * 128 to t * 128 + 127); the first is the block's own tile b.
All inputs are finite; a program needn't handle non-finite values.
Results may differ from the reference program's by a relative error of at most 0.022.
Values may be sent and summed in bfloat16 or wider, within the bound.
A program may use at most 128 MiB of HBM per device.

```python
import jax
import jax.numpy as jnp
from jax import lax

TILE = 128
KEPT = 40
BLK_DEV = 2
NB = 16384
NOCC = 1024
AUX = 24
ROWS = 1024


def draw_tile_ids(key, part):
    blocks = ROWS // TILE
    tile_total = NB // TILE
    random_keys = jax.random.randint(key, (blocks, tile_total), 0, 1 << 20)
    scores = random_keys * tile_total + jnp.arange(tile_total, dtype=jnp.int32)[None, :]
    own_tile = jnp.arange(blocks, dtype=jnp.int32)[:, None] == jnp.arange(tile_total, dtype=jnp.int32)[None, :]
    scores = jnp.where(own_tile, 1 << 30, scores)
    _, chosen = lax.top_k(scores, KEPT)
    return chosen.astype(jnp.int32)


def block_scale(key, extent, split, low, top_value):
    factor_of, own = 1.0, jax.random.fold_in(key, 6)
    for axis_at, shards_of in split:
        steps = jnp.exp(jax.random.uniform(jax.random.fold_in(own, axis_at), (shards_of,), jnp.float32, low / len(split), top_value / len(split)))
        factor_of = factor_of * jnp.repeat(steps, extent[axis_at] // shards_of).reshape([-1 if axis == axis_at else 1 for axis in range(len(extent))])
    return factor_of


def scatter_about(rng, dims, width, reach, split=(), held_as=jnp.bfloat16):
    level = block_scale(rng, dims, split, -0.22, 0.18) if split else 1.0
    values = jax.random.normal(rng, dims, jnp.float32) * width * level
    return jnp.minimum(jnp.maximum(values, -reach), reach).astype(held_as)


def setup_inputs(seed: int = 0) -> dict:
    key_list = jax.random.split(jax.random.key(seed), 5)
    integrals = scatter_about(key_list[0], (AUX, ROWS, KEPT * TILE), 1.0, 6.0, ((0, 8), (1, 4)))
    tile_ids = draw_tile_ids(jax.random.fold_in(key_list[4], 71), 0)
    coefficients = scatter_about(key_list[2], (NOCC, NB), (KEPT * TILE) ** -0.5, 0.078125, ((0, 8),))
    metric = scatter_about(key_list[3], (AUX, AUX), (AUX * AUX * NOCC) ** -0.5, 0.0078125, (), jnp.float32)
    return dict(integrals=integrals, tile_ids=tile_ids, coefficients=coefficients, metric=metric)


def reference(integrals, tile_ids, coefficients, metric):
    group_rows = BLK_DEV * TILE
    groups = ROWS // group_rows
    blocked = coefficients.reshape(NOCC, NB // TILE, TILE)

    def one_group(running, group_index):
        row_slab = lax.dynamic_slice_in_dim(integrals, group_index * group_rows, group_rows, 1)
        row_slab = row_slab.reshape(AUX, BLK_DEV, TILE, KEPT * TILE)
        group_ids = lax.dynamic_slice_in_dim(tile_ids, group_index * BLK_DEV, BLK_DEV, 0)
        picked = jnp.take(blocked, group_ids.reshape(BLK_DEV * KEPT), axis=1).reshape(NOCC, BLK_DEV, KEPT * TILE)
        halves = jnp.einsum("pbmk,jbk->pjbm", row_slab.astype(jnp.float32), picked.astype(jnp.float32))
        halves = halves.reshape(AUX, NOCC, group_rows).astype(jnp.bfloat16)
        halves = lax.optimization_barrier(halves)
        own_rows = lax.dynamic_slice_in_dim(coefficients, group_index * group_rows, group_rows, 1)
        partial_group = jnp.einsum("qjm,im->qji", halves.astype(jnp.float32), own_rows.astype(jnp.float32)).astype(jnp.bfloat16)
        partial_group = lax.optimization_barrier(partial_group)
        return running + partial_group.astype(jnp.float32), halves

    zeros_init = jnp.zeros((AUX, NOCC, NOCC), jnp.float32)
    occupied, halves_all = lax.scan(one_group, zeros_init, jnp.arange(groups, dtype=jnp.int32))
    fitted = jnp.einsum("pq,qji->pji", metric, occupied, precision=lax.Precision.HIGHEST).astype(jnp.bfloat16)
    fitted = lax.optimization_barrier(fitted)
    fitted_wide = fitted.astype(jnp.float32)

    def columns(group_index):
        return jnp.einsum("pjm,pji->im", halves_all[group_index].astype(jnp.float32), fitted_wide)

    column_blocks = lax.map(columns, jnp.arange(groups, dtype=jnp.int32))
    return jnp.transpose(column_blocks, (1, 0, 2)).reshape(NOCC, ROWS)
```

```python
import functools

import jax
import jax.numpy as jnp
from jax import lax
from jax.experimental import pallas as pl
from jax.experimental.pallas import tpu as pltpu
from jax.sharding import PartitionSpec as P


def pick_kernel(count, tile, ids_ref, coef_ref, out_ref, sem):
    def begin(slot, carry):
        source = pl.ds(pl.multiple_of(ids_ref[slot] * tile, tile), tile)
        target = pl.ds(pl.multiple_of(slot * tile, tile), tile)
        pltpu.make_async_copy(coef_ref.at[:, source], out_ref.at[:, target], sem).start()
        return carry

    lax.fori_loop(0, count, begin, 0)
    pltpu.make_async_copy(coef_ref.at[:, pl.ds(0, count * tile)], out_ref, sem).wait()


def pick(coefficients, ids, tile):
    count = ids.shape[0]
    return pl.pallas_call(
        functools.partial(pick_kernel, count, tile),
        out_shape=jax.ShapeDtypeStruct((coefficients.shape[0], count * tile), coefficients.dtype),
        in_specs=[
            pl.BlockSpec(memory_space=pltpu.SMEM),
            pl.BlockSpec(memory_space=pl.ANY),
        ],
        out_specs=pl.BlockSpec(memory_space=pltpu.VMEM),
        scratch_shapes=[pltpu.SemaphoreType.DMA],
    )(ids, coefficients)


MESH = pl.DeviceIdType.MESH
CORES = 2
SPLIT = 2
OWNERS = 2


def greet(peers):
    barrier = pltpu.get_barrier_semaphore()
    for peer in peers:
        pl.semaphore_signal(barrier, inc=1, device_id=peer, device_id_type=MESH)
    pl.semaphore_wait(barrier, len(peers))


def remote(source, target, send, recv, device):
    return pltpu.make_async_remote_copy(
        src_ref=source,
        dst_ref=target,
        send_sem=send,
        recv_sem=recv,
        device_id=device,
        device_id_type=MESH,
    )


def exchange_kernel(dims, ids_ref, metric_ref, coef_ref, ints_ref, out_ref, *scratch):
    rows, chips, orb_local, tile, count, aux_local, blocks, part = dims
    piece = orb_local // rows // SPLIT
    group = piece * rows
    routes = [(d, s) for d in range(1, chips) for s in (1, -1)]
    scratch = list(scratch)
    raw = {}
    for route in range(len(routes)):
        for h in range(SPLIT):
            raw[route, h] = scratch.pop(0)
    own, first_rows, kept, staged, both, ready, ids_v, ids_s = scratch[:8]
    parts, weight, crossed, mixed, total_ref = scratch[8:13]
    gram, part0, sum0, part1, sum1, part2, share, full, window_ref = scratch[13:22]
    z_send, z_recv, p_send, p_recv, l_sem, i_send, i_recv, x_send, x_recv = scratch[22:31]
    q_send, q_recv = scratch[31:33]
    send0, recv0, send1, recv1, send2, recv2, send3, recv3 = scratch[33:]
    width = count * tile // blocks
    total = rows * chips
    owners = rows * OWNERS
    row = lax.axis_index("row")
    orb = lax.axis_index("orb")
    chip = orb // CORES
    core = orb % CORES
    row_peers = [(lax.rem(row + t, rows), orb) for t in range(1, rows)]
    partner = (row, chip * CORES + 1 - core)
    me = row * chips + chip
    side_of = chip // 2
    mate = chip + 1 - 2 * (chip % 2)
    owner = (chip > 0) & (chip < chips - 1)
    home = row * OWNERS + side_of

    def place(k):
        other = lax.rem(me + k, total)
        return (other // chips, lax.rem(other, chips) * CORES + core)

    greet([place(k) for k in range(1, total)] + [partner])

    window = pltpu.make_async_copy(
        coef_ref.at[:, pl.ds(0, window_ref.shape[1])], window_ref, l_sem.at[4]
    )

    def z_copy(route, h, device):
        return remote(
            first_rows.at[h] if routes[route][0] == 1 else raw[route - 2, h],
            raw[route, h],
            z_send.at[route, h],
            z_recv.at[route, h],
            device,
        )

    def inside(where):
        return (where >= 0) & (where < chips)

    def towards(route, h):
        d, s = routes[route]
        there = chip + s
        valid = inside(there) & inside(chip - s * (d - 1))
        if d == 1 and h == SPLIT - 1:
            valid = valid & inside(there + s)
        return there, valid

    def origin(route):
        d, s = routes[route]
        there = chip - s * d
        return there, inside(there)

    tiles = own.shape[0]

    def every(source_rows, target, sem, act):
        def some(index, carry):
            at = pl.ds(pl.multiple_of(index * tile, tile), tile)
            act(pltpu.make_async_copy(coef_ref.at[source_rows, at], target.at[index], sem))
            return carry

        lax.fori_loop(0, tiles, some, 0)

    def first_piece(h, act):
        start = pl.multiple_of(h * group + row * piece, piece)
        every(pl.ds(start, piece), first_rows.at[h], l_sem.at[5 + h], act)

    all_rows = pl.ds(0, orb_local)
    for h in range(SPLIT):
        first_piece(h, lambda copy: copy.start())
    id_copies = []
    for t in range(1, rows):
        id_copies.append(
            remote(ids_ref, ids_v.at[t], i_send.at[t], i_recv.at[t], row_peers[t - 1])
        )
        id_copies[-1].start()

    for h in range(SPLIT):
        first_piece(h, lambda copy: copy.wait())
        for route in range(2):
            there, valid = towards(route, h)

            @pl.when(valid)
            def _():
                z_copy(route, h, (row, there * CORES + core)).start()

    every(all_rows, own, l_sem.at[0], lambda copy: copy.start())
    swap = remote(ints_ref, both.at[1], i_send.at[0], i_recv.at[0], partner)
    swap.start()
    bring = pltpu.make_async_copy(ints_ref, both.at[0], l_sem.at[2])
    bring.start()
    window.start()
    first = pltpu.make_async_copy(ids_ref, ids_s.at[0], l_sem.at[1])
    first.start()
    first.wait()
    for t in range(1, rows):
        id_copies[t - 1].wait()
        move = pltpu.make_async_copy(ids_v.at[t], ids_s.at[t], l_sem.at[1])
        move.start()
        move.wait()

    def take(source, targets, t):
        step = 8

        def some(block, carry):
            for k in range(step):
                slot = block * step + k
                at = pl.ds(pl.multiple_of(slot * tile, tile), tile)
                value = source[ids_s[t, 0, slot]]
                height = value.shape[0] // len(targets)
                for n, target in enumerate(targets):
                    target[:, at] = value[n * height : (n + 1) * height]
            return carry

        lax.fori_loop(0, count // step, some, 0)

    def band(from_row):
        return pl.ds(pl.multiple_of(from_row * piece, piece), piece)

    def spread(from_row, came, h, t, device):
        k = lax.rem(came + chips - chip, chips) - 1
        return remote(
            staged.at[k, h, t - 1],
            kept.at[came, h, band(from_row), :],
            p_send.at[k, h, t],
            p_recv.at[k, h, t],
            device,
        )

    direct = remote(
        kept.at[chip, SPLIT - 1],
        kept.at[chip, SPLIT - 1],
        q_send,
        q_recv,
        (row, mate * CORES + core),
    )

    def handout(came, h, k):
        to = lax.rem(home + k, owners)
        return remote(
            ready.at[came, h, to],
            parts.at[came, h, row, chip],
            x_send.at[came, h, k],
            x_recv.at[came, h, me],
            (to // OWNERS, (1 + lax.rem(to, OWNERS)) * CORES + core),
        )

    def keep(came, h):
        return pltpu.make_async_copy(
            ready.at[came, h, home], parts.at[came, h, row, chip], x_send.at[came, h, 0]
        )

    def product(came, h):
        def one(step, carry):
            side = step // blocks
            block = step - side * blocks
            slot = (core + side - 2 * core * side) * aux_local
            lhs = kept[came, h, :, pl.ds(pl.multiple_of(block * width, width), width)]
            at = pl.ds(pl.multiple_of(block * tile, tile), tile)
            rhs = both[side, :, at, :].reshape(aux_local * tile, width)
            result = lax.dot_general(
                lhs, rhs, (((1,), (1,)), ((), ())), preferred_element_type=jnp.float32
            )
            for p in range(aux_local):
                value = result[:, p * tile : (p + 1) * tile].astype(ready.dtype)
                ready[came, h, :, slot + p, :, at] = value.reshape(owners, part, tile)
            return carry

        lax.fori_loop(0, CORES * blocks, one, 0)

        @pl.when(owner)
        def _():
            keep(came, h).start()

        @pl.when(jnp.logical_not(owner))
        def _():
            handout(came, h, 0).start()

        for k in range(1, owners):
            handout(came, h, k).start()

    every(all_rows, own, l_sem.at[0], lambda copy: copy.wait())
    take(own, [kept.at[chip, h] for h in range(SPLIT)], 0)

    @pl.when(jnp.logical_not(owner))
    def _():
        direct.start()

    def pass_on(d):
        for h in range(SPLIT):
            for route in range(len(routes)):
                if routes[route][0] != d:
                    continue
                s = routes[route][1]
                came, valid = origin(route)
                special = d == 1 and h == SPLIT - 1

                @pl.when(valid & inside(chip + s) if special else valid)
                def _():
                    z_copy(route, h, partner).wait_recv()
                    if d + 1 < chips:
                        there, onward = towards(route + 2, h)

                        @pl.when(onward)
                        def _():
                            z_copy(route + 2, h, (row, there * CORES + core)).start()

                @pl.when(valid & (came != mate) if special else valid)
                def _():
                    k = lax.rem(came + chips - chip, chips) - 1
                    for t in range(1, rows):
                        take(raw[route, h], [staged.at[k, h, t - 1]], t)
                        spread(row, came, h, t, row_peers[rows - t - 1]).start()
                    take(raw[route, h], [kept.at[came, h, band(row), :]], 0)

    def multiply(d):
        for h in range(SPLIT):
            for route in range(len(routes)):
                if routes[route][0] != d:
                    continue
                came, valid = origin(route)
                special = d == 1 and h == SPLIT - 1

                @pl.when(valid & (came != mate) if special else valid)
                def _():
                    for t in range(1, rows):
                        source_row = lax.rem(row + t, rows)
                        spread(source_row, came, h, t, row_peers[0]).wait_recv()
                    product(came, h)

    def multiply_direct():
        remote(
            kept.at[mate, SPLIT - 1], kept.at[mate, SPLIT - 1], q_send, q_recv, partner
        ).wait_recv()
        product(mate, SPLIT - 1)

    def prepare():
        height = weight.shape[1]
        aux = metric_ref.shape[0]
        at = lax.broadcasted_iota(jnp.int32, (height, aux), 0)
        which = lax.broadcasted_iota(jnp.int32, (height, aux), 1)
        expand = jnp.where(at // part == which, 1.0, 0.0).astype(jnp.float32)
        left = lax.dot_general(
            expand,
            metric_ref[...],
            (((1,), (1,)), ((), ())),
            precision=lax.Precision.HIGHEST,
            preferred_element_type=jnp.float32,
        )
        wide = lax.dot_general(
            left,
            expand,
            (((1,), (1,)), ((), ())),
            precision=lax.Precision.HIGHEST,
            preferred_element_type=jnp.float32,
        )
        a = lax.broadcasted_iota(jnp.int32, (height, height), 0)
        b = lax.broadcasted_iota(jnp.int32, (height, height), 1)
        wide = jnp.where(a % part == b % part, wide, 0.0)
        high = wide.astype(weight.dtype)
        weight[0] = high
        weight[1] = (wide - high.astype(jnp.float32)).astype(weight.dtype)
        for r in range(rows):
            total_ref[r] = jnp.zeros(total_ref.shape[1:], jnp.float32)

    for d in range(1, chips):
        pass_on(d)
        if d == 1:
            bring.wait()
            swap.wait()
            for h in range(SPLIT):
                product(chip, h)
        if d == 2:

            @pl.when(owner)
            def _():
                direct.start()
                prepare()
                multiply_direct()

            multiply(1)

    multiply(2)

    @pl.when(jnp.logical_not(owner))
    def _():
        multiply_direct()

    multiply(3)

    def collect(came, h):
        def arrive(k, carry):
            source = lax.rem(me + k, total)
            remote(
                ready.at[came, h, 0],
                parts.at[came, h, source // chips, lax.rem(source, chips)],
                x_send.at[came, h, 0],
                x_recv.at[came, h, source],
                partner,
            ).wait_recv()
            return carry

        lax.fori_loop(1, total, arrive, 0)
        keep(came, h).wait()
        height = weight.shape[1]
        local = mixed.shape[2]
        for r in range(rows):
            value = parts[came, h, r].astype(jnp.float32).reshape(height, local)
            value = value.astype(mixed.dtype)
            result = jnp.dot(weight[0], value, preferred_element_type=jnp.float32)
            result = result + jnp.dot(weight[1], value, preferred_element_type=jnp.float32)
            mixed[r] = result.astype(mixed.dtype)
            crossed[r * local : (r + 1) * local, :] = value.T

        def add(r, carry):
            total_ref[r] += jnp.dot(
                crossed[...], mixed[r], preferred_element_type=jnp.float32
            )
            return carry

        lax.fori_loop(0, rows, add, 0)

    height = share.shape[0]
    half = height * OWNERS
    first_copies, second_copies, last_copies = [], [], []
    order = [lax.rem(row + t, rows) for t in range(1, rows)] + [row]
    near = 1 + side_of
    far = OWNERS - side_of
    for t, peer in enumerate(order):
        first_copies.append(
            remote(gram.at[peer], part0.at[peer], send0.at[t], recv0.at[t], partner)
        )
        if t < rows - 1:
            second_copies.append(
                remote(sum0.at[peer], part1.at[t], send1.at[t], recv1.at[t], (peer, orb))
            )
    third = remote(
        sum1.at[1 - side_of], part2, send2, recv2, (row, far * CORES + core)
    )

    def block(from_core, from_side):
        start = pl.multiple_of(from_core * half + from_side * height, height)
        return full.at[pl.ds(start, height), :]

    own_block = block(core, side_of)
    for n, device in enumerate(
        [
            (row, far * CORES + core),
            (row, mate * CORES + core),
            (row, (chips - 1 - mate) * CORES + core),
        ]
    ):
        last_copies.append(
            remote(share, own_block, send3.at[n], recv3.at[0, side_of], device)
        )
    last_copies.append(remote(share, own_block, send3.at[3], recv3.at[1, side_of], partner))

    def relay(side, n):
        return remote(
            block(core, side), block(core, side), send3.at[n], recv3.at[1, side], partner
        )

    def landed(from_core, side, kind):
        remote(
            share, block(from_core, side), send3.at[0], recv3.at[kind, side], partner
        ).wait_recv()

    mine_half = pl.ds(pl.multiple_of(core * half, half), half)
    other_half = pl.ds(pl.multiple_of((1 - core) * half, half), half)

    @pl.when(owner)
    def _():
        def early(u, carry):
            collect(1 + u // SPLIT, lax.rem(u, SPLIT))
            return carry

        def late(u, carry):
            collect((chips - 1) * (1 - lax.rem(u, 2)), u // 2)
            return carry

        lax.fori_loop(0, OWNERS * SPLIT, early, 0)
        lax.fori_loop(0, 2 * SPLIT, late, 0)
        for t, peer in enumerate(order):
            gram[peer] = total_ref[peer, other_half].astype(gram.dtype)
            first_copies[t].start()
        for t, peer in enumerate(order):
            first_copies[t].wait_recv()
            value = total_ref[peer, mine_half] + part0[peer].astype(jnp.float32)
            sum0[peer] = value.astype(sum0.dtype)
            if t < rows - 1:
                second_copies[t].start()
        for copy in second_copies:
            copy.wait_recv()
        value = sum0[row].astype(jnp.float32)
        for t in range(rows - 1):
            value = value + part1[t].astype(jnp.float32)
        sum1[...] = value.astype(sum1.dtype).reshape(sum1.shape)
        third.start()
        third.wait_recv()
        value = sum1[side_of].astype(jnp.float32) + part2[...].astype(jnp.float32)
        share[...] = value.astype(share.dtype)
        for copy in last_copies:
            copy.start()
        start = pl.multiple_of(core * half + side_of * height, height)
        full[pl.ds(start, height), :] = share[...]
        landed(core, 1 - side_of, 0)
        relay(1 - side_of, 4).start()

    @pl.when(jnp.logical_not(owner))
    def _():
        landed(core, side_of, 0)
        relay(side_of, 4).start()
        landed(core, 1 - side_of, 0)
        relay(1 - side_of, 5).start()

    window.wait()
    result = jnp.dot(
        window_ref[:, mine_half], full[mine_half, :], preferred_element_type=jnp.float32
    )
    for side in range(OWNERS):
        landed(1 - core, side, 1)
    out_ref[...] = result + jnp.dot(
        window_ref[:, other_half], full[other_half, :], preferred_element_type=jnp.float32
    )

    @pl.when(owner)
    def _():
        for copy in first_copies + second_copies + [third] + last_copies:
            copy.wait_send()
        relay(1 - side_of, 4).wait_send()

    @pl.when(jnp.logical_not(owner))
    def _():
        relay(side_of, 4).wait_send()
        relay(1 - side_of, 5).wait_send()

    direct.wait_send()
    for route in range(len(routes)):
        d = routes[route][0]
        came, valid = origin(route)
        for h in range(SPLIT):
            there, sent = towards(route, h)
            special = d == 1 and h == SPLIT - 1

            @pl.when(sent)
            def _():
                z_copy(route, h, (row, there * CORES + core)).wait_send()

            @pl.when(valid & (came != mate) if special else valid)
            def _():
                for t in range(1, rows):
                    spread(row, came, h, t, row_peers[rows - t - 1]).wait_send()

    for came in range(chips):
        for h in range(SPLIT):

            @pl.when(jnp.logical_not(owner))
            def _():
                handout(came, h, 0).wait_send()

            for k in range(1, owners):
                handout(came, h, k).wait_send()


def exchange(integrals, ids, coefficients, metric, rows, orbs, blocks, count):
    chips = orbs // CORES
    orb_local, basis = coefficients.shape
    aux_local, local_rows, _ = integrals.shape
    tile = local_rows // blocks
    owners = rows * OWNERS
    piece = orb_local // rows // SPLIT
    group = piece * rows
    part = group // owners
    aux = aux_local * orbs
    window = local_rows * rows
    half = window // CORES
    height = half // OWNERS
    routes = 2 * (chips - 1)
    dtype = coefficients.dtype
    scratch = [
        pltpu.VMEM((basis // tile, piece, tile), dtype) for _ in range(routes * SPLIT)
    ]
    scratch += [
        pltpu.VMEM((basis // tile, orb_local, tile), dtype),
        pltpu.VMEM((SPLIT, basis // tile, piece, tile), dtype),
        pltpu.VMEM((chips, SPLIT, group, count * tile), dtype),
        pltpu.VMEM((chips - 1, SPLIT, rows - 1, piece, count * tile), dtype),
        pltpu.VMEM((CORES,) + integrals.shape, dtype),
        pltpu.VMEM((chips, SPLIT, owners, CORES * aux_local, part, local_rows), dtype),
        pltpu.VMEM((rows, 1, ids.shape[1]), jnp.int32),
        pltpu.SMEM((rows, 1, ids.shape[1]), jnp.int32),
        pltpu.VMEM((chips, SPLIT, rows, chips, CORES * aux_local, part, local_rows), dtype),
        pltpu.VMEM((2, aux * part, aux * part), dtype),
        pltpu.VMEM((window, aux * part), dtype),
        pltpu.VMEM((rows, aux * part, local_rows), dtype),
        pltpu.VMEM((rows, window, local_rows), jnp.float32),
        pltpu.VMEM((rows, half, local_rows), dtype),
        pltpu.VMEM((rows, half, local_rows), dtype),
        pltpu.VMEM((rows, half, local_rows), dtype),
        pltpu.VMEM((rows - 1, half, local_rows), dtype),
        pltpu.VMEM((OWNERS, height, local_rows), dtype),
        pltpu.VMEM((height, local_rows), dtype),
        pltpu.VMEM((height, local_rows), dtype),
        pltpu.VMEM((window, local_rows), dtype),
        pltpu.VMEM((orb_local, window), dtype),
        pltpu.SemaphoreType.DMA((routes, SPLIT)),
        pltpu.SemaphoreType.DMA((routes, SPLIT)),
        pltpu.SemaphoreType.DMA((chips - 1, SPLIT, rows)),
        pltpu.SemaphoreType.DMA((chips - 1, SPLIT, rows)),
        pltpu.SemaphoreType.DMA((5 + SPLIT,)),
        pltpu.SemaphoreType.DMA((rows,)),
        pltpu.SemaphoreType.DMA((rows,)),
        pltpu.SemaphoreType.DMA((chips, SPLIT, owners)),
        pltpu.SemaphoreType.DMA((chips, SPLIT, rows * chips)),
        pltpu.SemaphoreType.DMA,
        pltpu.SemaphoreType.DMA,
        pltpu.SemaphoreType.DMA((rows,)),
        pltpu.SemaphoreType.DMA((rows,)),
        pltpu.SemaphoreType.DMA((rows,)),
        pltpu.SemaphoreType.DMA((rows,)),
        pltpu.SemaphoreType.DMA,
        pltpu.SemaphoreType.DMA,
        pltpu.SemaphoreType.DMA((6,)),
        pltpu.SemaphoreType.DMA((2, OWNERS)),
    ]
    dims = (rows, chips, orb_local, tile, count, aux_local, blocks, part)
    return pl.pallas_call(
        functools.partial(exchange_kernel, dims),
        out_shape=jax.ShapeDtypeStruct((orb_local, local_rows), jnp.float32),
        in_specs=[pl.BlockSpec(memory_space=pltpu.VMEM)] * 2
        + [pl.BlockSpec(memory_space=pl.ANY)] * 2,
        out_specs=pl.BlockSpec(memory_space=pltpu.VMEM),
        scratch_shapes=scratch,
        compiler_params=pltpu.CompilerParams(
            collective_id=0, has_side_effects=True, vmem_limit_bytes=63 << 20
        ),
    )(ids, metric, coefficients, integrals)


def per_device(rows, orbs, integrals, tile_ids, coefficients, metric):
    orb_local, basis_width = coefficients.shape
    block_count, kept_count = tile_ids.shape
    chips = orbs // CORES
    if (
        chips != 2 * OWNERS
        or orb_local % (16 * SPLIT * rows)
        or orb_local % (8 * SPLIT * OWNERS * rows)
        or block_count * kept_count % 8
    ):
        return plain_device(rows, orbs, integrals, tile_ids, coefficients, metric)
    count = block_count * kept_count
    lanes = -(-count // 128) * 128
    ids = jnp.pad(tile_ids.reshape(1, count), ((0, 0), (0, lanes - count)))
    return exchange(integrals, ids, coefficients, metric, rows, orbs, block_count, count)


def plain_device(rows, orbs, integrals, tile_ids, coefficients, metric):
    aux_local, local_rows, kept_width = integrals.shape
    orb_local, basis_width = coefficients.shape
    block_count, kept_count = tile_ids.shape
    tile_rows = local_rows // block_count
    orbitals = orb_local * orbs
    aux = aux_local * orbs
    window = local_rows * rows
    part = orbitals // (rows * orbs)
    picked = pick(coefficients, tile_ids.reshape(block_count * kept_count), tile_rows)
    col_piece = lax.all_gather(picked, "orb", axis=0, tiled=True)
    slabs = integrals.reshape(aux_local, block_count, tile_rows, kept_width)
    halves = [
        jnp.einsum(
            "pmk,jk->pjm",
            slabs[:, b],
            col_piece[:, b * kept_width : (b + 1) * kept_width],
            preferred_element_type=jnp.float32,
        ).astype(jnp.bfloat16)
        for b in range(block_count)
    ]
    halves = jnp.concatenate(halves, axis=2)
    outgoing = halves.reshape(aux_local, rows * orbs, part, local_rows).transpose(1, 0, 2, 3)
    by_part = lax.all_to_all(outgoing, ("row", "orb"), split_axis=0, concat_axis=0, tiled=True)
    by_part = by_part.reshape(rows, aux, part, local_rows)
    mixed = jnp.einsum(
        "pq,rpjm->rqjm", metric, by_part.astype(jnp.float32), precision=lax.Precision.HIGHEST
    ).astype(jnp.bfloat16)
    gram = jnp.einsum(
        "rqjm,sqjn->rmsn", by_part, mixed, preferred_element_type=jnp.float32
    ).astype(jnp.bfloat16)
    gram = gram.reshape(orbs, window // orbs, rows, local_rows).transpose(2, 0, 1, 3)
    gram = gram.reshape(rows * window, local_rows)
    share = lax.psum_scatter(gram, ("row", "orb"), scatter_dimension=0, tiled=True)
    columns = lax.all_gather(share, "orb", axis=0, tiled=True)
    return jnp.dot(coefficients[:, :window], columns, preferred_element_type=jnp.float32)


def solution(mesh):
    return jax.shard_map(
        functools.partial(per_device, mesh.shape["row"], mesh.shape["orb"]),
        mesh=mesh,
        in_specs=(P("orb", "row", None), P("row", None), P("orb", None), P()),
        out_specs=P("orb", "row"),
        check_vma=False,
    )
```

```python
import functools

import jax
import jax.numpy as jnp
from jax import lax
from jax.experimental import pallas as pl
from jax.experimental.pallas import tpu as pltpu
from jax.sharding import PartitionSpec as P


def pick_kernel(count, tile, ids_ref, coef_ref, out_ref, sem):
    def begin(slot, carry):
        source = pl.ds(pl.multiple_of(ids_ref[slot] * tile, tile), tile)
        target = pl.ds(pl.multiple_of(slot * tile, tile), tile)
        pltpu.make_async_copy(coef_ref.at[:, source], out_ref.at[:, target], sem).start()
        return carry

    lax.fori_loop(0, count, begin, 0)
    pltpu.make_async_copy(coef_ref.at[:, pl.ds(0, count * tile)], out_ref, sem).wait()


def pick(coefficients, ids, tile):
    count = ids.shape[0]
    return pl.pallas_call(
        functools.partial(pick_kernel, count, tile),
        out_shape=jax.ShapeDtypeStruct((coefficients.shape[0], count * tile), coefficients.dtype),
        in_specs=[
            pl.BlockSpec(memory_space=pltpu.SMEM),
            pl.BlockSpec(memory_space=pl.ANY),
        ],
        out_specs=pl.BlockSpec(memory_space=pltpu.VMEM),
        scratch_shapes=[pltpu.SemaphoreType.DMA],
    )(ids, coefficients)


MESH = pl.DeviceIdType.MESH
CORES = 2
SPLIT = 2
OWNERS = 2


def greet(peers):
    barrier = pltpu.get_barrier_semaphore()
    for peer in peers:
        pl.semaphore_signal(barrier, inc=1, device_id=peer, device_id_type=MESH)
    pl.semaphore_wait(barrier, len(peers))


def remote(source, target, send, recv, device):
    return pltpu.make_async_remote_copy(
        src_ref=source,
        dst_ref=target,
        send_sem=send,
        recv_sem=recv,
        device_id=device,
        device_id_type=MESH,
    )


def exchange_kernel(dims, ids_ref, metric_ref, coef_ref, ints_ref, out_ref, *scratch):
    rows, chips, orb_local, tile, count, aux_local, blocks, part = dims
    piece = orb_local // rows // SPLIT
    group = piece * rows
    routes = [(d, s) for d in range(1, chips) for s in (1, -1)]
    scratch = list(scratch)
    raw = {}
    for route in range(len(routes)):
        for h in range(SPLIT):
            raw[route, h] = scratch.pop(0)
    own, kept, staged, both, ready, ids_v, ids_s = scratch[:7]
    first_rows = scratch.pop()
    parts, weight, crossed, mixed, total_ref = scratch[7:12]
    gram, part0, sum0, part1, sum1, part2, share, full, window_ref = scratch[12:21]
    z_send, z_recv, p_send, p_recv, l_sem, i_send, i_recv, x_send, x_recv = scratch[21:30]
    q_send, q_recv, relayed, y_recv, y_send = scratch[30:35]
    send0, recv0, send1, recv1, send2, recv2, send3, recv3 = scratch[35:]
    width = count * tile // blocks
    total = rows * chips
    owners = rows * OWNERS
    row = lax.axis_index("row")
    orb = lax.axis_index("orb")
    chip = orb // CORES
    core = orb % CORES
    row_peers = [(lax.rem(row + t, rows), orb) for t in range(1, rows)]
    partner = (row, chip * CORES + 1 - core)
    me = row * chips + chip
    side_of = chip // 2
    mate = chip + 1 - 2 * (chip % 2)
    owner = (chip > 0) & (chip < chips - 1)
    home = row * OWNERS + side_of

    def place(k):
        other = lax.rem(me + k, total)
        return (other // chips, lax.rem(other, chips) * CORES + core)

    greet([place(k) for k in range(1, total)] + [partner])

    window = pltpu.make_async_copy(
        coef_ref.at[:, pl.ds(0, window_ref.shape[1])], window_ref, l_sem.at[4]
    )

    def z_copy(route, h, device):
        return remote(
            first_rows.at[h] if routes[route][0] == 1 else raw[route - 2, h],
            raw[route, h],
            z_send.at[route, h],
            z_recv.at[route, h],
            device,
        )

    def inside(where):
        return (where >= 0) & (where < chips)

    def towards(route, h):
        d, s = routes[route]
        there = chip + s
        valid = inside(there) & inside(chip - s * (d - 1))
        if d == 1 and h == SPLIT - 1:
            valid = valid & inside(there + s)
        return there, valid

    def origin(route):
        d, s = routes[route]
        there = chip - s * d
        return there, inside(there)

    tiles = own.shape[0]

    def every(source_rows, target, sem, act):
        step = 8

        def some(index, carry):
            for n in range(step):
                which = index * step + n
                at = pl.ds(pl.multiple_of(which * tile, tile), tile)
                act(pltpu.make_async_copy(coef_ref.at[source_rows, at], target.at[which], sem))
            return carry

        lax.fori_loop(0, tiles // step, some, 0)

    def first_piece(h, act):
        start = pl.multiple_of(h * group + row * piece, piece)
        every(pl.ds(start, piece), first_rows.at[h], l_sem.at[5 + h], act)

    all_rows = pl.ds(0, orb_local)
    for h in range(SPLIT):
        first_piece(h, lambda copy: copy.start())
    bring = pltpu.make_async_copy(ints_ref, both.at[0], l_sem.at[2])
    swap = remote(ints_ref, both.at[1], i_send.at[0], i_recv.at[0], partner)
    for h in range(SPLIT):
        first_piece(h, lambda copy: copy.wait())
        for route in range(2):
            there, valid = towards(route, h)

            @pl.when(valid)
            def _():
                z_copy(route, h, (row, there * CORES + core)).start()

    every(all_rows, own, l_sem.at[0], lambda copy: copy.start())
    bring.start()
    swap.start()
    id_copies = []
    for t in range(1, rows):
        id_copies.append(
            remote(ids_ref, ids_v.at[t], i_send.at[t], i_recv.at[t], row_peers[t - 1])
        )
        id_copies[-1].start()

    window.start()
    first = pltpu.make_async_copy(ids_ref, ids_s.at[0], l_sem.at[1])
    first.start()
    first.wait()
    for t in range(1, rows):
        id_copies[t - 1].wait()
        move = pltpu.make_async_copy(ids_v.at[t], ids_s.at[t], l_sem.at[1])
        move.start()
        move.wait()

    def take(source, targets, t):
        step = 8

        def some(block, carry):
            for k in range(step):
                slot = block * step + k
                at = pl.ds(pl.multiple_of(slot * tile, tile), tile)
                value = source[ids_s[t, 0, slot]]
                height = value.shape[0] // len(targets)
                for n, target in enumerate(targets):
                    target[:, at] = value[n * height : (n + 1) * height]
            return carry

        lax.fori_loop(0, count // step, some, 0)

    def band(from_row):
        return pl.ds(pl.multiple_of(from_row * piece, piece), piece)

    def spread(from_row, came, h, t, device):
        k = lax.rem(came + chips - chip, chips) - 1
        return remote(
            staged.at[k, h, t - 1],
            kept.at[came, h, band(from_row), :],
            p_send.at[k, h, t],
            p_recv.at[k, h, t],
            device,
        )

    direct = remote(
        kept.at[chip, SPLIT - 1],
        kept.at[chip, SPLIT - 1],
        q_send,
        q_recv,
        (row, mate * CORES + core),
    )

    whole = pl.ds(0, CORES * aux_local)

    def handout(came, h, k, some=whole):
        to = lax.rem(home + k, owners)
        return remote(
            ready.at[came, h, to, some],
            parts.at[came, h, row, chip, some],
            x_send.at[came, h, k],
            x_recv.at[came, h, me],
            (to // OWNERS, (1 + lax.rem(to, OWNERS)) * CORES + core),
        )

    def keep(came, h, some=whole):
        return pltpu.make_async_copy(
            ready.at[came, h, home, some],
            parts.at[came, h, row, chip, some],
            x_send.at[came, h, 0],
        )

    def along(came, h, side, some=whole):
        return remote(
            ready.at[came, h, row * OWNERS + side, some],
            parts.at[came, h, row, chip, some],
            x_send.at[came, h, side],
            x_recv.at[came, h, me],
            (row, (1 + side) * CORES + core),
        )

    def across(came, h, t, some=whole):
        to = lax.rem(row + t, rows)
        return remote(
            ready.at[came, h, pl.ds(to * OWNERS, OWNERS), some],
            relayed.at[came, h, t - 1, :, some],
            x_send.at[came, h, OWNERS + t],
            y_recv.at[came, h, t - 1],
            (to, orb),
        )

    def onwards(came, h, t, side):
        source = lax.rem(row + rows - t, rows)
        return remote(
            relayed.at[came, h, t - 1, side],
            parts.at[came, h, source, chip],
            y_send.at[came, h, t - 1, side],
            x_recv.at[came, h, source * chips + chip],
            (row, (1 + side) * CORES + core),
        )

    def hand(came, h, some=whole):
        @pl.when(owner)
        def _():
            keep(came, h, some).start()
            for k in range(1, owners):
                handout(came, h, k, some).start()

        @pl.when(jnp.logical_not(owner))
        def _():
            for t in range(1, rows):
                across(came, h, t, some).start()
            for side in range(OWNERS):
                along(came, h, side, some).start()

    def forward(came, h):
        for t in range(1, rows):
            across(came, h, t).wait_recv()
            for side in range(OWNERS):
                onwards(came, h, t, side).start()

    def slot_of(side):
        return (core + side - 2 * core * side) * aux_local

    def some_products(lhs_of, side, block, store):
        lhs = lhs_of(pl.ds(pl.multiple_of(block * width, width), width))
        at = pl.ds(pl.multiple_of(block * tile, tile), tile)
        rhs = both[side, :, at, :].reshape(aux_local * tile, width)
        result = lax.dot_general(
            lhs, rhs, (((1,), (1,)), ((), ())), preferred_element_type=jnp.float32
        )
        for p in range(aux_local):
            value = result[:, p * tile : (p + 1) * tile].astype(ready.dtype)
            store(slot_of(side) + p, at, value)

    def product(came, h):
        def one(step, carry):
            side = step // blocks

            def store(slot, at, value):
                ready[came, h, :, slot, :, at] = value.reshape(owners, part, tile)

            some_products(
                lambda at: kept[came, h, :, at], side, step - side * blocks, store
            )
            return carry

        lax.fori_loop(0, CORES * blocks, one, 0)

        hand(came, h)

    def own_product(side):
        def one(block, carry):
            def store(slot, at, value):
                for h in range(SPLIT):
                    rows_of_h = value[h * group : (h + 1) * group]
                    ready[chip, h, :, slot, :, at] = rows_of_h.reshape(owners, part, tile)

            some_products(
                lambda at: kept[chip, :, :, at].reshape(orb_local, width), side, block, store
            )
            return carry

        lax.fori_loop(0, blocks, one, 0)
        some = pl.ds(slot_of(side), aux_local)
        for h in range(SPLIT):
            hand(chip, h, some)

    every(all_rows, own, l_sem.at[0], lambda copy: copy.wait())
    take(own, [kept.at[chip, h] for h in range(SPLIT)], 0)

    @pl.when(jnp.logical_not(owner))
    def _():
        direct.start()

    def pass_on(d):
        for h in range(SPLIT):
            for route in range(len(routes)):
                if routes[route][0] != d:
                    continue
                s = routes[route][1]
                came, valid = origin(route)
                special = d == 1 and h == SPLIT - 1

                @pl.when(valid & inside(chip + s) if special else valid)
                def _():
                    z_copy(route, h, partner).wait_recv()
                    if d + 1 < chips:
                        there, onward = towards(route + 2, h)

                        @pl.when(onward)
                        def _():
                            z_copy(route + 2, h, (row, there * CORES + core)).start()

                @pl.when(valid & (came != mate) if special else valid)
                def _():
                    k = lax.rem(came + chips - chip, chips) - 1
                    for t in range(1, rows):
                        take(raw[route, h], [staged.at[k, h, t - 1]], t)
                        spread(row, came, h, t, row_peers[rows - t - 1]).start()
                    take(raw[route, h], [kept.at[came, h, band(row), :]], 0)

    def multiply(d, pieces=range(SPLIT)):
        for h in pieces:
            for route in range(len(routes)):
                if routes[route][0] != d:
                    continue
                came, valid = origin(route)
                special = d == 1 and h == SPLIT - 1

                @pl.when(valid & (came != mate) if special else valid)
                def _():
                    for t in range(1, rows):
                        source_row = lax.rem(row + t, rows)
                        spread(source_row, came, h, t, row_peers[0]).wait_recv()
                    product(came, h)

    def multiply_direct():
        remote(
            kept.at[mate, SPLIT - 1], kept.at[mate, SPLIT - 1], q_send, q_recv, partner
        ).wait_recv()
        product(mate, SPLIT - 1)

    def prepare():
        height = weight.shape[1]
        aux = metric_ref.shape[0]
        at = lax.broadcasted_iota(jnp.int32, (height, aux), 0)
        which = lax.broadcasted_iota(jnp.int32, (height, aux), 1)
        expand = jnp.where(at // part == which, 1.0, 0.0).astype(jnp.float32)
        left = lax.dot_general(
            expand,
            metric_ref[...],
            (((1,), (1,)), ((), ())),
            precision=lax.Precision.HIGHEST,
            preferred_element_type=jnp.float32,
        )
        wide = lax.dot_general(
            left,
            expand,
            (((1,), (1,)), ((), ())),
            precision=lax.Precision.HIGHEST,
            preferred_element_type=jnp.float32,
        )
        a = lax.broadcasted_iota(jnp.int32, (height, height), 0)
        b = lax.broadcasted_iota(jnp.int32, (height, height), 1)
        wide = jnp.where(a % part == b % part, wide, 0.0)
        high = wide.astype(weight.dtype)
        weight[0] = high
        weight[1] = (wide - high.astype(jnp.float32)).astype(weight.dtype)
        for r in range(rows):
            total_ref[r] = jnp.zeros(total_ref.shape[1:], jnp.float32)

    bring.wait()
    own_product(0)
    pass_on(1)
    swap.wait()
    own_product(1)
    pass_on(2)

    @pl.when(owner)
    def _():
        direct.start()
        prepare()

    multiply(1)

    @pl.when(owner)
    def _():
        multiply_direct()

    pass_on(3)
    end = jnp.logical_not(owner)
    inward = 1 - 2 * side_of

    @pl.when(end)
    def _():
        for h in range(SPLIT):
            forward(chip, h)
        forward(mate, 0)

    multiply(2)
    multiply(3, [0])

    @pl.when(end)
    def _():
        for h in range(SPLIT):
            forward(chip + 2 * inward, h)
        multiply_direct()
        forward(chip + 3 * inward, 0)

    multiply(3, [1])

    @pl.when(end)
    def _():
        forward(mate, SPLIT - 1)
        forward(chip + 3 * inward, SPLIT - 1)

    def collect(came, h):
        def arrive(k, carry):
            source = lax.rem(me + k, total)
            remote(
                ready.at[came, h, 0],
                parts.at[came, h, source // chips, lax.rem(source, chips)],
                x_send.at[came, h, 0],
                x_recv.at[came, h, source],
                partner,
            ).wait_recv()
            return carry

        lax.fori_loop(1, total, arrive, 0)
        keep(came, h).wait()
        height = weight.shape[1]
        local = mixed.shape[2]
        for r in range(rows):
            value = parts[came, h, r].astype(jnp.float32).reshape(height, local)
            value = value.astype(mixed.dtype)
            result = jnp.dot(weight[0], value, preferred_element_type=jnp.float32)
            result = result + jnp.dot(weight[1], value, preferred_element_type=jnp.float32)
            mixed[r] = result.astype(mixed.dtype)
            crossed[r * local : (r + 1) * local, :] = value.T

        def add(r, carry):
            total_ref[r] += jnp.dot(
                crossed[...], mixed[r], preferred_element_type=jnp.float32
            )
            return carry

        lax.fori_loop(0, rows, add, 0)

    height = share.shape[0]
    half = height * OWNERS
    first_copies, second_copies, last_copies = [], [], []
    order = [lax.rem(row + t, rows) for t in range(1, rows)] + [row]
    near = 1 + side_of
    far = OWNERS - side_of
    for t, peer in enumerate(order):
        first_copies.append(
            remote(gram.at[peer], part0.at[peer], send0.at[t], recv0.at[t], partner)
        )
        if t < rows - 1:
            second_copies.append(
                remote(sum0.at[peer], part1.at[t], send1.at[t], recv1.at[t], (peer, orb))
            )
    third = remote(
        sum1.at[1 - side_of], part2, send2, recv2, (row, far * CORES + core)
    )

    def block(from_core, from_side):
        start = pl.multiple_of(from_core * half + from_side * height, height)
        return full.at[pl.ds(start, height), :]

    own_block = block(core, side_of)
    for n, device in enumerate(
        [
            (row, far * CORES + core),
            (row, mate * CORES + core),
            (row, (chips - 1 - mate) * CORES + core),
        ]
    ):
        last_copies.append(
            remote(share, own_block, send3.at[n], recv3.at[0, side_of], device)
        )
    last_copies.append(remote(share, own_block, send3.at[3], recv3.at[1, side_of], partner))

    def relay(side, n):
        return remote(
            block(core, side), block(core, side), send3.at[n], recv3.at[1, side], partner
        )

    def landed(from_core, side, kind):
        remote(
            share, block(from_core, side), send3.at[0], recv3.at[kind, side], partner
        ).wait_recv()

    mine_half = pl.ds(pl.multiple_of(core * half, half), half)
    other_half = pl.ds(pl.multiple_of((1 - core) * half, half), half)

    @pl.when(owner)
    def _():
        def inner(u, carry):
            collect(1 + lax.rem(u, 2), u // 2)
            return carry

        def outer(u, carry):
            collect((chips - 1) * lax.rem(u, 2), u // 2)
            return carry

        for h in range(SPLIT):
            lax.fori_loop(h * OWNERS, (h + 1) * OWNERS, inner, 0)
            lax.fori_loop(h * OWNERS, (h + 1) * OWNERS, outer, 0)
        for t, peer in enumerate(order):
            gram[peer] = total_ref[peer, other_half].astype(gram.dtype)
            first_copies[t].start()
        for t, peer in enumerate(order):
            first_copies[t].wait_recv()
            value = total_ref[peer, mine_half] + part0[peer].astype(jnp.float32)
            sum0[peer] = value.astype(sum0.dtype)
            if t < rows - 1:
                second_copies[t].start()
        for copy in second_copies:
            copy.wait_recv()
        value = sum0[row].astype(jnp.float32)
        for t in range(rows - 1):
            value = value + part1[t].astype(jnp.float32)
        sum1[...] = value.astype(sum1.dtype).reshape(sum1.shape)
        third.start()
        third.wait_recv()
        value = sum1[side_of].astype(jnp.float32) + part2[...].astype(jnp.float32)
        share[...] = value.astype(share.dtype)
        for copy in last_copies:
            copy.start()
        start = pl.multiple_of(core * half + side_of * height, height)
        full[pl.ds(start, height), :] = share[...]
        landed(core, 1 - side_of, 0)
        relay(1 - side_of, 4).start()

    @pl.when(jnp.logical_not(owner))
    def _():
        landed(core, side_of, 0)
        relay(side_of, 4).start()
        landed(core, 1 - side_of, 0)
        relay(1 - side_of, 5).start()

    window.wait()
    result = jnp.dot(
        window_ref[:, mine_half], full[mine_half, :], preferred_element_type=jnp.float32
    )
    for side in range(OWNERS):
        landed(1 - core, side, 1)
    out_ref[...] = result + jnp.dot(
        window_ref[:, other_half], full[other_half, :], preferred_element_type=jnp.float32
    )

    @pl.when(owner)
    def _():
        for copy in first_copies + second_copies + [third] + last_copies:
            copy.wait_send()
        relay(1 - side_of, 4).wait_send()

    @pl.when(jnp.logical_not(owner))
    def _():
        relay(side_of, 4).wait_send()
        relay(1 - side_of, 5).wait_send()

    direct.wait_send()
    for route in range(len(routes)):
        d = routes[route][0]
        came, valid = origin(route)
        for h in range(SPLIT):
            there, sent = towards(route, h)
            special = d == 1 and h == SPLIT - 1

            @pl.when(sent)
            def _():
                z_copy(route, h, (row, there * CORES + core)).wait_send()

            @pl.when(valid & (came != mate) if special else valid)
            def _():
                for t in range(1, rows):
                    spread(row, came, h, t, row_peers[rows - t - 1]).wait_send()

    for came in range(chips):
        for h in range(SPLIT):

            @pl.when(owner)
            def _():
                for k in range(1, owners):
                    handout(came, h, k).wait_send()

            @pl.when(jnp.logical_not(owner))
            def _():
                for side in range(OWNERS):
                    along(came, h, side).wait_send()
                for t in range(1, rows):
                    across(came, h, t).wait_send()
                    for side in range(OWNERS):
                        onwards(came, h, t, side).wait_send()


def exchange(integrals, ids, coefficients, metric, rows, orbs, blocks, count):
    chips = orbs // CORES
    orb_local, basis = coefficients.shape
    aux_local, local_rows, _ = integrals.shape
    tile = local_rows // blocks
    owners = rows * OWNERS
    piece = orb_local // rows // SPLIT
    group = piece * rows
    part = group // owners
    aux = aux_local * orbs
    window = local_rows * rows
    half = window // CORES
    height = half // OWNERS
    routes = 2 * (chips - 1)
    dtype = coefficients.dtype
    scratch = [
        pltpu.VMEM((basis // tile, piece, tile), dtype) for _ in range(routes * SPLIT)
    ]
    scratch += [
        pltpu.VMEM((basis // tile, orb_local, tile), dtype),
        pltpu.VMEM((chips, SPLIT, group, count * tile), dtype),
        pltpu.VMEM((chips - 1, SPLIT, rows - 1, piece, count * tile), dtype),
        pltpu.VMEM((CORES,) + integrals.shape, dtype),
        pltpu.VMEM((chips, SPLIT, owners, CORES * aux_local, part, local_rows), dtype),
        pltpu.VMEM((rows, 1, ids.shape[1]), jnp.int32),
        pltpu.SMEM((rows, 1, ids.shape[1]), jnp.int32),
        pltpu.VMEM((chips, SPLIT, rows, chips, CORES * aux_local, part, local_rows), dtype),
        pltpu.VMEM((2, aux * part, aux * part), dtype),
        pltpu.VMEM((window, aux * part), dtype),
        pltpu.VMEM((rows, aux * part, local_rows), dtype),
        pltpu.VMEM((rows, window, local_rows), jnp.float32),
        pltpu.VMEM((rows, half, local_rows), dtype),
        pltpu.VMEM((rows, half, local_rows), dtype),
        pltpu.VMEM((rows, half, local_rows), dtype),
        pltpu.VMEM((rows - 1, half, local_rows), dtype),
        pltpu.VMEM((OWNERS, height, local_rows), dtype),
        pltpu.VMEM((height, local_rows), dtype),
        pltpu.VMEM((height, local_rows), dtype),
        pltpu.VMEM((window, local_rows), dtype),
        pltpu.VMEM((orb_local, window), dtype),
        pltpu.SemaphoreType.DMA((routes, SPLIT)),
        pltpu.SemaphoreType.DMA((routes, SPLIT)),
        pltpu.SemaphoreType.DMA((chips - 1, SPLIT, rows)),
        pltpu.SemaphoreType.DMA((chips - 1, SPLIT, rows)),
        pltpu.SemaphoreType.DMA((5 + SPLIT,)),
        pltpu.SemaphoreType.DMA((rows,)),
        pltpu.SemaphoreType.DMA((rows,)),
        pltpu.SemaphoreType.DMA((chips, SPLIT, owners)),
        pltpu.SemaphoreType.DMA((chips, SPLIT, rows * chips)),
        pltpu.SemaphoreType.DMA,
        pltpu.SemaphoreType.DMA,
        pltpu.VMEM(
            (chips, SPLIT, rows - 1, OWNERS, CORES * aux_local, part, local_rows), dtype
        ),
        pltpu.SemaphoreType.DMA((chips, SPLIT, rows - 1)),
        pltpu.SemaphoreType.DMA((chips, SPLIT, rows - 1, OWNERS)),
        pltpu.SemaphoreType.DMA((rows,)),
        pltpu.SemaphoreType.DMA((rows,)),
        pltpu.SemaphoreType.DMA((rows,)),
        pltpu.SemaphoreType.DMA((rows,)),
        pltpu.SemaphoreType.DMA,
        pltpu.SemaphoreType.DMA,
        pltpu.SemaphoreType.DMA((6,)),
        pltpu.SemaphoreType.DMA((2, OWNERS)),
        pltpu.VMEM((SPLIT, basis // tile, piece, tile), dtype),
    ]
    dims = (rows, chips, orb_local, tile, count, aux_local, blocks, part)
    return pl.pallas_call(
        functools.partial(exchange_kernel, dims),
        out_shape=jax.ShapeDtypeStruct((orb_local, local_rows), jnp.float32),
        in_specs=[pl.BlockSpec(memory_space=pltpu.VMEM)] * 2
        + [pl.BlockSpec(memory_space=pl.ANY)] * 2,
        out_specs=pl.BlockSpec(memory_space=pltpu.VMEM),
        scratch_shapes=scratch,
        compiler_params=pltpu.CompilerParams(
            collective_id=0, has_side_effects=True, vmem_limit_bytes=63 << 20
        ),
    )(ids, metric, coefficients, integrals)


def per_device(rows, orbs, integrals, tile_ids, coefficients, metric):
    orb_local, basis_width = coefficients.shape
    block_count, kept_count = tile_ids.shape
    chips = orbs // CORES
    if (
        chips != 2 * OWNERS
        or orb_local % (16 * SPLIT * rows)
        or orb_local % (8 * SPLIT * OWNERS * rows)
        or block_count * kept_count % 8
        or basis_width // (integrals.shape[1] // block_count) % 8
    ):
        return plain_device(rows, orbs, integrals, tile_ids, coefficients, metric)
    count = block_count * kept_count
    lanes = -(-count // 128) * 128
    ids = jnp.pad(tile_ids.reshape(1, count), ((0, 0), (0, lanes - count)))
    return exchange(integrals, ids, coefficients, metric, rows, orbs, block_count, count)


def plain_device(rows, orbs, integrals, tile_ids, coefficients, metric):
    aux_local, local_rows, kept_width = integrals.shape
    orb_local, basis_width = coefficients.shape
    block_count, kept_count = tile_ids.shape
    tile_rows = local_rows // block_count
    orbitals = orb_local * orbs
    aux = aux_local * orbs
    window = local_rows * rows
    part = orbitals // (rows * orbs)
    picked = pick(coefficients, tile_ids.reshape(block_count * kept_count), tile_rows)
    col_piece = lax.all_gather(picked, "orb", axis=0, tiled=True)
    slabs = integrals.reshape(aux_local, block_count, tile_rows, kept_width)
    halves = [
        jnp.einsum(
            "pmk,jk->pjm",
            slabs[:, b],
            col_piece[:, b * kept_width : (b + 1) * kept_width],
            preferred_element_type=jnp.float32,
        ).astype(jnp.bfloat16)
        for b in range(block_count)
    ]
    halves = jnp.concatenate(halves, axis=2)
    outgoing = halves.reshape(aux_local, rows * orbs, part, local_rows).transpose(1, 0, 2, 3)
    by_part = lax.all_to_all(outgoing, ("row", "orb"), split_axis=0, concat_axis=0, tiled=True)
    by_part = by_part.reshape(rows, aux, part, local_rows)
    mixed = jnp.einsum(
        "pq,rpjm->rqjm", metric, by_part.astype(jnp.float32), precision=lax.Precision.HIGHEST
    ).astype(jnp.bfloat16)
    gram = jnp.einsum(
        "rqjm,sqjn->rmsn", by_part, mixed, preferred_element_type=jnp.float32
    ).astype(jnp.bfloat16)
    gram = gram.reshape(orbs, window // orbs, rows, local_rows).transpose(2, 0, 1, 3)
    gram = gram.reshape(rows * window, local_rows)
    share = lax.psum_scatter(gram, ("row", "orb"), scatter_dimension=0, tiled=True)
    columns = lax.all_gather(share, "orb", axis=0, tiled=True)
    return jnp.dot(coefficients[:, :window], columns, preferred_element_type=jnp.float32)


def solution(mesh):
    return jax.shard_map(
        functools.partial(per_device, mesh.shape["row"], mesh.shape["orb"]),
        mesh=mesh,
        in_specs=(P("orb", "row", None), P("row", None), P("orb", None), P()),
        out_specs=P("orb", "row"),
        check_vma=False,
    )
```

```python
import functools

import jax
import jax.numpy as jnp
from jax import lax
from jax.experimental import pallas as pl
from jax.experimental.pallas import tpu as pltpu
from jax.sharding import PartitionSpec as P


def pick_kernel(count, tile, ids_ref, coef_ref, out_ref, sem):
    def begin(slot, carry):
        source = pl.ds(pl.multiple_of(ids_ref[slot] * tile, tile), tile)
        target = pl.ds(pl.multiple_of(slot * tile, tile), tile)
        pltpu.make_async_copy(coef_ref.at[:, source], out_ref.at[:, target], sem).start()
        return carry

    lax.fori_loop(0, count, begin, 0)
    pltpu.make_async_copy(coef_ref.at[:, pl.ds(0, count * tile)], out_ref, sem).wait()


def pick(coefficients, ids, tile):
    count = ids.shape[0]
    return pl.pallas_call(
        functools.partial(pick_kernel, count, tile),
        out_shape=jax.ShapeDtypeStruct((coefficients.shape[0], count * tile), coefficients.dtype),
        in_specs=[
            pl.BlockSpec(memory_space=pltpu.SMEM),
            pl.BlockSpec(memory_space=pl.ANY),
        ],
        out_specs=pl.BlockSpec(memory_space=pltpu.VMEM),
        scratch_shapes=[pltpu.SemaphoreType.DMA],
    )(ids, coefficients)


MESH = pl.DeviceIdType.MESH
CORES = 2
SPLIT = 2
OWNERS = 2


def greet(peers):
    barrier = pltpu.get_barrier_semaphore()
    for peer in peers:
        pl.semaphore_signal(barrier, inc=1, device_id=peer, device_id_type=MESH)
    pl.semaphore_wait(barrier, len(peers))


def remote(source, target, send, recv, device):
    return pltpu.make_async_remote_copy(
        src_ref=source,
        dst_ref=target,
        send_sem=send,
        recv_sem=recv,
        device_id=device,
        device_id_type=MESH,
    )


def exchange_kernel(dims, ids_ref, metric_ref, coef_ref, ints_ref, out_ref, *scratch):
    rows, chips, orb_local, tile, count, aux_local, blocks, part = dims
    piece = orb_local // rows // SPLIT
    group = piece * rows
    routes = [(d, s) for d in range(1, chips) for s in (1, -1)]
    scratch = list(scratch)
    raw = {}
    for route in range(len(routes)):
        for h in range(SPLIT):
            raw[route, h] = scratch.pop(0)
    own, kept, staged, both, ready, ids_v, ids_s = scratch[:7]
    first_rows = scratch.pop()
    partz, sumz, partb, sendz, recvz, sendb, recvb = scratch[-7:]
    scratch = scratch[:-7]
    parts, weight, crossed, mixed, total_ref = scratch[7:12]
    gram, part0, sum0, part1, sum1, part2, share, full, window_ref = scratch[12:21]
    z_send, z_recv, p_send, p_recv, l_sem, i_send, i_recv, x_send, x_recv = scratch[21:30]
    q_send, q_recv, relayed, y_recv, y_send = scratch[30:35]
    send0, recv0, send1, recv1, send2, recv2, send3, recv3 = scratch[35:]
    width = count * tile // blocks
    total = rows * chips
    owners = rows * OWNERS
    row = lax.axis_index("row")
    orb = lax.axis_index("orb")
    chip = orb // CORES
    core = orb % CORES
    row_peers = [(lax.rem(row + t, rows), orb) for t in range(1, rows)]
    partner = (row, chip * CORES + 1 - core)
    me = row * chips + chip
    side_of = chip // 2
    mate = chip + 1 - 2 * (chip % 2)
    owner = (chip > 0) & (chip < chips - 1)
    home = row * OWNERS + side_of

    def place(k):
        other = lax.rem(me + k, total)
        return (other // chips, lax.rem(other, chips) * CORES + core)

    greet([place(k) for k in range(1, total)] + [partner])

    window = pltpu.make_async_copy(
        coef_ref.at[:, pl.ds(0, window_ref.shape[1])], window_ref, l_sem.at[4]
    )

    def z_copy(route, h, device):
        return remote(
            first_rows.at[h] if routes[route][0] == 1 else raw[route - 2, h],
            raw[route, h],
            z_send.at[route, h],
            z_recv.at[route, h],
            device,
        )

    def inside(where):
        return (where >= 0) & (where < chips)

    def towards(route, h):
        d, s = routes[route]
        there = chip + s
        valid = inside(there) & inside(chip - s * (d - 1))
        if d == 1 and h == SPLIT - 1:
            valid = valid & inside(there + s)
        return there, valid

    def origin(route):
        d, s = routes[route]
        there = chip - s * d
        return there, inside(there)

    tiles = own.shape[0]

    def every(source_rows, target, sem, act):
        step = 8

        def some(index, carry):
            for n in range(step):
                which = index * step + n
                at = pl.ds(pl.multiple_of(which * tile, tile), tile)
                act(pltpu.make_async_copy(coef_ref.at[source_rows, at], target.at[which], sem))
            return carry

        lax.fori_loop(0, tiles // step, some, 0)

    def first_piece(h, act):
        start = pl.multiple_of(h * group + row * piece, piece)
        every(pl.ds(start, piece), first_rows.at[h], l_sem.at[5 + h], act)

    all_rows = pl.ds(0, orb_local)
    for h in range(SPLIT):
        first_piece(h, lambda copy: copy.start())
    bring = pltpu.make_async_copy(ints_ref, both.at[0], l_sem.at[2])
    swap = remote(ints_ref, both.at[1], i_send.at[0], i_recv.at[0], partner)
    for h in range(SPLIT):
        first_piece(h, lambda copy: copy.wait())
        for route in range(2):
            there, valid = towards(route, h)

            @pl.when(valid)
            def _():
                z_copy(route, h, (row, there * CORES + core)).start()

    every(all_rows, own, l_sem.at[0], lambda copy: copy.start())
    bring.start()
    swap.start()
    id_copies = []
    for t in range(1, rows):
        id_copies.append(
            remote(ids_ref, ids_v.at[t], i_send.at[t], i_recv.at[t], row_peers[t - 1])
        )
        id_copies[-1].start()

    window.start()
    first = pltpu.make_async_copy(ids_ref, ids_s.at[0], l_sem.at[1])
    first.start()
    first.wait()
    for t in range(1, rows):
        id_copies[t - 1].wait()
        move = pltpu.make_async_copy(ids_v.at[t], ids_s.at[t], l_sem.at[1])
        move.start()
        move.wait()

    def take(source, targets, t):
        step = 8

        def some(block, carry):
            for k in range(step):
                slot = block * step + k
                at = pl.ds(pl.multiple_of(slot * tile, tile), tile)
                value = source[ids_s[t, 0, slot]]
                height = value.shape[0] // len(targets)
                for n, target in enumerate(targets):
                    target[:, at] = value[n * height : (n + 1) * height]
            return carry

        lax.fori_loop(0, count // step, some, 0)

    def band(from_row):
        return pl.ds(pl.multiple_of(from_row * piece, piece), piece)

    def spread(from_row, came, h, t, device):
        k = lax.rem(came + chips - chip, chips) - 1
        return remote(
            staged.at[k, h, t - 1],
            kept.at[came, h, band(from_row), :],
            p_send.at[k, h, t],
            p_recv.at[k, h, t],
            device,
        )

    direct = remote(
        kept.at[chip, SPLIT - 1],
        kept.at[chip, SPLIT - 1],
        q_send,
        q_recv,
        (row, mate * CORES + core),
    )

    whole = pl.ds(0, CORES * aux_local)

    def handout(came, h, k, some=whole):
        to = lax.rem(home + k, owners)
        return remote(
            ready.at[came, h, to, some],
            parts.at[came, h, row, chip, some],
            x_send.at[came, h, k],
            x_recv.at[came, h, me],
            (to // OWNERS, (1 + lax.rem(to, OWNERS)) * CORES + core),
        )

    def keep(came, h, some=whole):
        return pltpu.make_async_copy(
            ready.at[came, h, home, some],
            parts.at[came, h, row, chip, some],
            x_send.at[came, h, 0],
        )

    def along(came, h, side, some=whole):
        return remote(
            ready.at[came, h, row * OWNERS + side, some],
            parts.at[came, h, row, chip, some],
            x_send.at[came, h, side],
            x_recv.at[came, h, me],
            (row, (1 + side) * CORES + core),
        )

    def across(came, h, t, some=whole):
        to = lax.rem(row + t, rows)
        return remote(
            ready.at[came, h, pl.ds(to * OWNERS, OWNERS), some],
            relayed.at[came, h, t - 1, :, some],
            x_send.at[came, h, OWNERS + t],
            y_recv.at[came, h, t - 1],
            (to, orb),
        )

    def onwards(came, h, t, side):
        source = lax.rem(row + rows - t, rows)
        return remote(
            relayed.at[came, h, t - 1, side],
            parts.at[came, h, source, chip],
            y_send.at[came, h, t - 1, side],
            x_recv.at[came, h, source * chips + chip],
            (row, (1 + side) * CORES + core),
        )

    def hand(came, h, some=whole):
        @pl.when(owner)
        def _():
            keep(came, h, some).start()
            for k in range(1, owners):
                handout(came, h, k, some).start()

        @pl.when(jnp.logical_not(owner))
        def _():
            for t in range(1, rows):
                across(came, h, t, some).start()
            for side in range(OWNERS):
                along(came, h, side, some).start()

    def forward(came, h):
        for t in range(1, rows):
            across(came, h, t).wait_recv()
            for side in range(OWNERS):
                onwards(came, h, t, side).start()

    def slot_of(side):
        return (core + side - 2 * core * side) * aux_local

    def some_products(lhs_of, side, block, store):
        lhs = lhs_of(pl.ds(pl.multiple_of(block * width, width), width))
        at = pl.ds(pl.multiple_of(block * tile, tile), tile)
        rhs = both[side, :, at, :].reshape(aux_local * tile, width)
        result = lax.dot_general(
            lhs, rhs, (((1,), (1,)), ((), ())), preferred_element_type=jnp.float32
        )
        for p in range(aux_local):
            value = result[:, p * tile : (p + 1) * tile].astype(ready.dtype)
            store(slot_of(side) + p, at, value)

    def product(came, h):
        def one(step, carry):
            side = step // blocks

            def store(slot, at, value):
                ready[came, h, :, slot, :, at] = value.reshape(owners, part, tile)

            some_products(
                lambda at: kept[came, h, :, at], side, step - side * blocks, store
            )
            return carry

        lax.fori_loop(0, CORES * blocks, one, 0)

        hand(came, h)

    def own_product(side):
        def one(block, carry):
            def store(slot, at, value):
                for h in range(SPLIT):
                    rows_of_h = value[h * group : (h + 1) * group]
                    ready[chip, h, :, slot, :, at] = rows_of_h.reshape(owners, part, tile)

            some_products(
                lambda at: kept[chip, :, :, at].reshape(orb_local, width), side, block, store
            )
            return carry

        lax.fori_loop(0, blocks, one, 0)
        some = pl.ds(slot_of(side), aux_local)
        for h in range(SPLIT):
            hand(chip, h, some)

    every(all_rows, own, l_sem.at[0], lambda copy: copy.wait())
    take(own, [kept.at[chip, h] for h in range(SPLIT)], 0)

    @pl.when(jnp.logical_not(owner))
    def _():
        direct.start()

    def pass_on(d):
        for h in range(SPLIT):
            for route in range(len(routes)):
                if routes[route][0] != d:
                    continue
                s = routes[route][1]
                came, valid = origin(route)
                special = d == 1 and h == SPLIT - 1

                @pl.when(valid & inside(chip + s) if special else valid)
                def _():
                    z_copy(route, h, partner).wait_recv()
                    if d + 1 < chips:
                        there, onward = towards(route + 2, h)

                        @pl.when(onward)
                        def _():
                            z_copy(route + 2, h, (row, there * CORES + core)).start()

                @pl.when(valid & (came != mate) if special else valid)
                def _():
                    k = lax.rem(came + chips - chip, chips) - 1
                    for t in range(1, rows):
                        take(raw[route, h], [staged.at[k, h, t - 1]], t)
                        spread(row, came, h, t, row_peers[rows - t - 1]).start()
                    take(raw[route, h], [kept.at[came, h, band(row), :]], 0)

    def multiply(d, pieces=range(SPLIT)):
        for h in pieces:
            for route in range(len(routes)):
                if routes[route][0] != d:
                    continue
                came, valid = origin(route)
                special = d == 1 and h == SPLIT - 1

                @pl.when(valid & (came != mate) if special else valid)
                def _():
                    for t in range(1, rows):
                        source_row = lax.rem(row + t, rows)
                        spread(source_row, came, h, t, row_peers[0]).wait_recv()
                    product(came, h)

    def multiply_direct():
        remote(
            kept.at[mate, SPLIT - 1], kept.at[mate, SPLIT - 1], q_send, q_recv, partner
        ).wait_recv()
        product(mate, SPLIT - 1)

    def prepare():
        height = weight.shape[1]
        aux = metric_ref.shape[0]
        at = lax.broadcasted_iota(jnp.int32, (height, aux), 0)
        which = lax.broadcasted_iota(jnp.int32, (height, aux), 1)
        expand = jnp.where(at // part == which, 1.0, 0.0).astype(jnp.float32)
        left = lax.dot_general(
            expand,
            metric_ref[...],
            (((1,), (1,)), ((), ())),
            precision=lax.Precision.HIGHEST,
            preferred_element_type=jnp.float32,
        )
        wide = lax.dot_general(
            left,
            expand,
            (((1,), (1,)), ((), ())),
            precision=lax.Precision.HIGHEST,
            preferred_element_type=jnp.float32,
        )
        a = lax.broadcasted_iota(jnp.int32, (height, height), 0)
        b = lax.broadcasted_iota(jnp.int32, (height, height), 1)
        wide = jnp.where(a % part == b % part, wide, 0.0)
        high = wide.astype(weight.dtype)
        weight[0] = high
        weight[1] = (wide - high.astype(jnp.float32)).astype(weight.dtype)
        for r in range(rows):
            total_ref[r] = jnp.zeros(total_ref.shape[1:], jnp.float32)

    bring.wait()
    own_product(0)
    pass_on(1)
    swap.wait()
    own_product(1)
    pass_on(2)

    @pl.when(owner)
    def _():
        direct.start()
        prepare()

    multiply(1)

    @pl.when(owner)
    def _():
        multiply_direct()

    pass_on(3)
    end = jnp.logical_not(owner)
    inward = 1 - 2 * side_of

    @pl.when(end)
    def _():
        for h in range(SPLIT):
            forward(chip, h)
        forward(mate, 0)

    multiply(2)
    multiply(3, [0])

    @pl.when(end)
    def _():
        for h in range(SPLIT):
            forward(chip + 2 * inward, h)
        multiply_direct()
        forward(chip + 3 * inward, 0)

    multiply(3, [1])

    @pl.when(end)
    def _():
        forward(mate, SPLIT - 1)
        forward(chip + 3 * inward, SPLIT - 1)

    def collect(came, h):
        def arrive(k, carry):
            source = lax.rem(me + k, total)
            remote(
                ready.at[came, h, 0],
                parts.at[came, h, source // chips, lax.rem(source, chips)],
                x_send.at[came, h, 0],
                x_recv.at[came, h, source],
                partner,
            ).wait_recv()
            return carry

        lax.fori_loop(1, total, arrive, 0)
        keep(came, h).wait()
        height = weight.shape[1]
        local = mixed.shape[2]
        for r in range(rows):
            value = parts[came, h, r].astype(jnp.float32).reshape(height, local)
            value = value.astype(mixed.dtype)
            result = jnp.dot(weight[0], value, preferred_element_type=jnp.float32)
            result = result + jnp.dot(weight[1], value, preferred_element_type=jnp.float32)
            mixed[r] = result.astype(mixed.dtype)
            crossed[r * local : (r + 1) * local, :] = value.T

        def add(r, carry):
            total_ref[r] += jnp.dot(
                crossed[...], mixed[r], preferred_element_type=jnp.float32
            )
            return carry

        lax.fori_loop(0, rows, add, 0)

    height = share.shape[0]
    half = height * OWNERS
    quarter = height // 2
    first_copies, second_copies, last_copies = [], [], []
    across_copies, after_copies = [], []
    order = [lax.rem(row + t, rows) for t in range(1, rows)] + [row]
    near = 1 + side_of
    far = OWNERS - side_of
    for t, peer in enumerate(order):
        first_copies.append(
            remote(gram.at[peer], part0.at[peer], send0.at[t], recv0.at[t], partner)
        )
        start = pl.multiple_of((1 - side_of) * height + quarter, quarter)
        across_copies.append(
            remote(
                sum0.at[peer, pl.ds(start, quarter)],
                partz.at[peer],
                sendz.at[t],
                recvz.at[t],
                (row, far * CORES + core),
            )
        )
        if t < rows - 1:
            second_copies.append(
                [
                    remote(
                        sum0.at[peer, pl.ds(side * height, quarter)],
                        part1.at[t, side],
                        send1.at[t, side],
                        recv1.at[t, side],
                        (peer, orb),
                    )
                    for side in range(OWNERS)
                ]
            )
            after_copies.append(
                remote(sumz.at[peer], partb.at[t], sendb.at[t], recvb.at[t], (peer, orb))
            )
    third = remote(
        sum1.at[1 - side_of], part2, send2, recv2, (row, far * CORES + core)
    )

    def block(from_core, from_side):
        start = pl.multiple_of(from_core * half + from_side * height, height)
        return full.at[pl.ds(start, height), :]

    own_block = block(core, side_of)
    for n, device in enumerate(
        [
            (row, far * CORES + core),
            (row, mate * CORES + core),
            (row, (chips - 1 - mate) * CORES + core),
        ]
    ):
        last_copies.append(
            remote(share, own_block, send3.at[n], recv3.at[0, side_of], device)
        )
    last_copies.append(remote(share, own_block, send3.at[3], recv3.at[1, side_of], partner))

    def relay(side, n):
        return remote(
            block(core, side), block(core, side), send3.at[n], recv3.at[1, side], partner
        )

    def landed(from_core, side, kind):
        remote(
            share, block(from_core, side), send3.at[0], recv3.at[kind, side], partner
        ).wait_recv()

    mine_half = pl.ds(pl.multiple_of(core * half, half), half)
    other_half = pl.ds(pl.multiple_of((1 - core) * half, half), half)

    @pl.when(owner)
    def _():
        def inner(u, carry):
            collect(1 + lax.rem(u, 2), u // 2)
            return carry

        def outer(u, carry):
            collect((chips - 1) * lax.rem(u, 2), u // 2)
            return carry

        for h in range(SPLIT):
            lax.fori_loop(h * OWNERS, (h + 1) * OWNERS, inner, 0)
            lax.fori_loop(h * OWNERS, (h + 1) * OWNERS, outer, 0)
        for t, peer in enumerate(order):
            gram[peer] = total_ref[peer, other_half].astype(gram.dtype)
            first_copies[t].start()
        for t, peer in enumerate(order):
            first_copies[t].wait_recv()
            value = total_ref[peer, mine_half] + part0[peer].astype(jnp.float32)
            sum0[peer] = value.astype(sum0.dtype)
            across_copies[t].start()
            if t < rows - 1:
                for copy in second_copies[t]:
                    copy.start()
        for t, peer in enumerate(order):
            across_copies[t].wait_recv()
            start = pl.multiple_of(side_of * height + quarter, quarter)
            value = sum0[peer, pl.ds(start, quarter)].astype(jnp.float32)
            sumz[peer] = (value + partz[peer].astype(jnp.float32)).astype(sumz.dtype)
            if t < rows - 1:
                after_copies[t].start()
        for copies in second_copies:
            for copy in copies:
                copy.wait_recv()
        for side in range(OWNERS):
            value = sum0[row, side * height : side * height + quarter].astype(jnp.float32)
            for t in range(rows - 1):
                value = value + part1[t, side].astype(jnp.float32)
            sum1[side] = value.astype(sum1.dtype)
        third.start()
        for copy in after_copies:
            copy.wait_recv()
        value = sumz[row].astype(jnp.float32)
        for t in range(rows - 1):
            value = value + partb[t].astype(jnp.float32)
        share[quarter:] = value.astype(share.dtype)
        third.wait_recv()
        value = sum1[side_of].astype(jnp.float32) + part2[...].astype(jnp.float32)
        share[:quarter] = value.astype(share.dtype)
        for copy in last_copies:
            copy.start()
        start = pl.multiple_of(core * half + side_of * height, height)
        full[pl.ds(start, height), :] = share[...]
        landed(core, 1 - side_of, 0)
        relay(1 - side_of, 4).start()

    @pl.when(jnp.logical_not(owner))
    def _():
        landed(core, side_of, 0)
        relay(side_of, 4).start()
        landed(core, 1 - side_of, 0)
        relay(1 - side_of, 5).start()

    window.wait()
    result = jnp.dot(
        window_ref[:, mine_half], full[mine_half, :], preferred_element_type=jnp.float32
    )
    for side in range(OWNERS):
        landed(1 - core, side, 1)
    out_ref[...] = result + jnp.dot(
        window_ref[:, other_half], full[other_half, :], preferred_element_type=jnp.float32
    )

    @pl.when(owner)
    def _():
        for copy in sum(second_copies, first_copies + across_copies + after_copies):
            copy.wait_send()
        for copy in [third] + last_copies:
            copy.wait_send()
        relay(1 - side_of, 4).wait_send()

    @pl.when(jnp.logical_not(owner))
    def _():
        relay(side_of, 4).wait_send()
        relay(1 - side_of, 5).wait_send()

    direct.wait_send()
    for route in range(len(routes)):
        d = routes[route][0]
        came, valid = origin(route)
        for h in range(SPLIT):
            there, sent = towards(route, h)
            special = d == 1 and h == SPLIT - 1

            @pl.when(sent)
            def _():
                z_copy(route, h, (row, there * CORES + core)).wait_send()

            @pl.when(valid & (came != mate) if special else valid)
            def _():
                for t in range(1, rows):
                    spread(row, came, h, t, row_peers[rows - t - 1]).wait_send()

    for came in range(chips):
        for h in range(SPLIT):

            @pl.when(owner)
            def _():
                for k in range(1, owners):
                    handout(came, h, k).wait_send()

            @pl.when(jnp.logical_not(owner))
            def _():
                for side in range(OWNERS):
                    along(came, h, side).wait_send()
                for t in range(1, rows):
                    across(came, h, t).wait_send()
                    for side in range(OWNERS):
                        onwards(came, h, t, side).wait_send()


def exchange(integrals, ids, coefficients, metric, rows, orbs, blocks, count):
    chips = orbs // CORES
    orb_local, basis = coefficients.shape
    aux_local, local_rows, _ = integrals.shape
    tile = local_rows // blocks
    owners = rows * OWNERS
    piece = orb_local // rows // SPLIT
    group = piece * rows
    part = group // owners
    aux = aux_local * orbs
    window = local_rows * rows
    half = window // CORES
    height = half // OWNERS
    quarter = height // 2
    routes = 2 * (chips - 1)
    dtype = coefficients.dtype
    scratch = [
        pltpu.VMEM((basis // tile, piece, tile), dtype) for _ in range(routes * SPLIT)
    ]
    scratch += [
        pltpu.VMEM((basis // tile, orb_local, tile), dtype),
        pltpu.VMEM((chips, SPLIT, group, count * tile), dtype),
        pltpu.VMEM((chips - 1, SPLIT, rows - 1, piece, count * tile), dtype),
        pltpu.VMEM((CORES,) + integrals.shape, dtype),
        pltpu.VMEM((chips, SPLIT, owners, CORES * aux_local, part, local_rows), dtype),
        pltpu.VMEM((rows, 1, ids.shape[1]), jnp.int32),
        pltpu.SMEM((rows, 1, ids.shape[1]), jnp.int32),
        pltpu.VMEM((chips, SPLIT, rows, chips, CORES * aux_local, part, local_rows), dtype),
        pltpu.VMEM((2, aux * part, aux * part), dtype),
        pltpu.VMEM((window, aux * part), dtype),
        pltpu.VMEM((rows, aux * part, local_rows), dtype),
        pltpu.VMEM((rows, window, local_rows), jnp.float32),
        pltpu.VMEM((rows, half, local_rows), dtype),
        pltpu.VMEM((rows, half, local_rows), dtype),
        pltpu.VMEM((rows, half, local_rows), dtype),
        pltpu.VMEM((rows - 1, OWNERS, quarter, local_rows), dtype),
        pltpu.VMEM((OWNERS, quarter, local_rows), dtype),
        pltpu.VMEM((quarter, local_rows), dtype),
        pltpu.VMEM((height, local_rows), dtype),
        pltpu.VMEM((window, local_rows), dtype),
        pltpu.VMEM((orb_local, window), dtype),
        pltpu.SemaphoreType.DMA((routes, SPLIT)),
        pltpu.SemaphoreType.DMA((routes, SPLIT)),
        pltpu.SemaphoreType.DMA((chips - 1, SPLIT, rows)),
        pltpu.SemaphoreType.DMA((chips - 1, SPLIT, rows)),
        pltpu.SemaphoreType.DMA((5 + SPLIT,)),
        pltpu.SemaphoreType.DMA((rows,)),
        pltpu.SemaphoreType.DMA((rows,)),
        pltpu.SemaphoreType.DMA((chips, SPLIT, owners)),
        pltpu.SemaphoreType.DMA((chips, SPLIT, rows * chips)),
        pltpu.SemaphoreType.DMA,
        pltpu.SemaphoreType.DMA,
        pltpu.VMEM(
            (chips, SPLIT, rows - 1, OWNERS, CORES * aux_local, part, local_rows), dtype
        ),
        pltpu.SemaphoreType.DMA((chips, SPLIT, rows - 1)),
        pltpu.SemaphoreType.DMA((chips, SPLIT, rows - 1, OWNERS)),
        pltpu.SemaphoreType.DMA((rows,)),
        pltpu.SemaphoreType.DMA((rows,)),
        pltpu.SemaphoreType.DMA((rows, OWNERS)),
        pltpu.SemaphoreType.DMA((rows, OWNERS)),
        pltpu.SemaphoreType.DMA,
        pltpu.SemaphoreType.DMA,
        pltpu.SemaphoreType.DMA((6,)),
        pltpu.SemaphoreType.DMA((2, OWNERS)),
        pltpu.VMEM((rows, quarter, local_rows), dtype),
        pltpu.VMEM((rows, quarter, local_rows), dtype),
        pltpu.VMEM((rows - 1, quarter, local_rows), dtype),
        pltpu.SemaphoreType.DMA((rows,)),
        pltpu.SemaphoreType.DMA((rows,)),
        pltpu.SemaphoreType.DMA((rows,)),
        pltpu.SemaphoreType.DMA((rows,)),
        pltpu.VMEM((SPLIT, basis // tile, piece, tile), dtype),
    ]
    dims = (rows, chips, orb_local, tile, count, aux_local, blocks, part)
    return pl.pallas_call(
        functools.partial(exchange_kernel, dims),
        out_shape=jax.ShapeDtypeStruct((orb_local, local_rows), jnp.float32),
        in_specs=[pl.BlockSpec(memory_space=pltpu.VMEM)] * 2
        + [pl.BlockSpec(memory_space=pl.ANY)] * 2,
        out_specs=pl.BlockSpec(memory_space=pltpu.VMEM),
        scratch_shapes=scratch,
        compiler_params=pltpu.CompilerParams(
            collective_id=0, has_side_effects=True, vmem_limit_bytes=63 << 20
        ),
    )(ids, metric, coefficients, integrals)


def per_device(rows, orbs, integrals, tile_ids, coefficients, metric):
    orb_local, basis_width = coefficients.shape
    block_count, kept_count = tile_ids.shape
    chips = orbs // CORES
    if (
        chips != 2 * OWNERS
        or orb_local % (16 * SPLIT * rows)
        or orb_local % (8 * SPLIT * OWNERS * rows)
        or block_count * kept_count % 8
        or basis_width // (integrals.shape[1] // block_count) % 8
    ):
        return plain_device(rows, orbs, integrals, tile_ids, coefficients, metric)
    count = block_count * kept_count
    lanes = -(-count // 128) * 128
    ids = jnp.pad(tile_ids.reshape(1, count), ((0, 0), (0, lanes - count)))
    return exchange(integrals, ids, coefficients, metric, rows, orbs, block_count, count)


def plain_device(rows, orbs, integrals, tile_ids, coefficients, metric):
    aux_local, local_rows, kept_width = integrals.shape
    orb_local, basis_width = coefficients.shape
    block_count, kept_count = tile_ids.shape
    tile_rows = local_rows // block_count
    orbitals = orb_local * orbs
    aux = aux_local * orbs
    window = local_rows * rows
    part = orbitals // (rows * orbs)
    picked = pick(coefficients, tile_ids.reshape(block_count * kept_count), tile_rows)
    col_piece = lax.all_gather(picked, "orb", axis=0, tiled=True)
    slabs = integrals.reshape(aux_local, block_count, tile_rows, kept_width)
    halves = [
        jnp.einsum(
            "pmk,jk->pjm",
            slabs[:, b],
            col_piece[:, b * kept_width : (b + 1) * kept_width],
            preferred_element_type=jnp.float32,
        ).astype(jnp.bfloat16)
        for b in range(block_count)
    ]
    halves = jnp.concatenate(halves, axis=2)
    outgoing = halves.reshape(aux_local, rows * orbs, part, local_rows).transpose(1, 0, 2, 3)
    by_part = lax.all_to_all(outgoing, ("row", "orb"), split_axis=0, concat_axis=0, tiled=True)
    by_part = by_part.reshape(rows, aux, part, local_rows)
    mixed = jnp.einsum(
        "pq,rpjm->rqjm", metric, by_part.astype(jnp.float32), precision=lax.Precision.HIGHEST
    ).astype(jnp.bfloat16)
    gram = jnp.einsum(
        "rqjm,sqjn->rmsn", by_part, mixed, preferred_element_type=jnp.float32
    ).astype(jnp.bfloat16)
    gram = gram.reshape(orbs, window // orbs, rows, local_rows).transpose(2, 0, 1, 3)
    gram = gram.reshape(rows * window, local_rows)
    share = lax.psum_scatter(gram, ("row", "orb"), scatter_dimension=0, tiled=True)
    columns = lax.all_gather(share, "orb", axis=0, tiled=True)
    return jnp.dot(coefficients[:, :window], columns, preferred_element_type=jnp.float32)


def solution(mesh):
    return jax.shard_map(
        functools.partial(per_device, mesh.shape["row"], mesh.shape["orb"]),
        mesh=mesh,
        in_specs=(P("orb", "row", None), P("row", None), P("orb", None), P()),
        out_specs=P("orb", "row"),
        check_vma=False,
    )
```

```python
import functools

import jax
import jax.numpy as jnp
from jax import lax
from jax.experimental import pallas as pl
from jax.experimental.pallas import tpu as pltpu
from jax.sharding import PartitionSpec as P


def pick_kernel(count, tile, ids_ref, coef_ref, out_ref, sem):
    def begin(slot, carry):
        source = pl.ds(pl.multiple_of(ids_ref[slot] * tile, tile), tile)
        target = pl.ds(pl.multiple_of(slot * tile, tile), tile)
        pltpu.make_async_copy(coef_ref.at[:, source], out_ref.at[:, target], sem).start()
        return carry

    lax.fori_loop(0, count, begin, 0)
    pltpu.make_async_copy(coef_ref.at[:, pl.ds(0, count * tile)], out_ref, sem).wait()


def pick(coefficients, ids, tile):
    count = ids.shape[0]
    return pl.pallas_call(
        functools.partial(pick_kernel, count, tile),
        out_shape=jax.ShapeDtypeStruct((coefficients.shape[0], count * tile), coefficients.dtype),
        in_specs=[
            pl.BlockSpec(memory_space=pltpu.SMEM),
            pl.BlockSpec(memory_space=pl.ANY),
        ],
        out_specs=pl.BlockSpec(memory_space=pltpu.VMEM),
        scratch_shapes=[pltpu.SemaphoreType.DMA],
    )(ids, coefficients)


MESH = pl.DeviceIdType.MESH
CORES = 2
SPLIT = 2
OWNERS = 2


def greet(peers):
    barrier = pltpu.get_barrier_semaphore()
    for peer in peers:
        pl.semaphore_signal(barrier, inc=1, device_id=peer, device_id_type=MESH)
    pl.semaphore_wait(barrier, len(peers))


def remote(source, target, send, recv, device):
    return pltpu.make_async_remote_copy(
        src_ref=source,
        dst_ref=target,
        send_sem=send,
        recv_sem=recv,
        device_id=device,
        device_id_type=MESH,
    )


def exchange_kernel(dims, ids_ref, metric_ref, coef_ref, ints_ref, out_ref, *scratch):
    rows, chips, orb_local, tile, count, aux_local, blocks, part = dims
    piece = orb_local // rows // SPLIT
    group = piece * rows
    routes = [(d, s) for d in range(1, chips) for s in (1, -1)]
    scratch = list(scratch)
    raw = {}
    for route in range(len(routes)):
        for h in range(SPLIT):
            raw[route, h] = scratch.pop(0)
    own, kept, staged, both, ready, ids_v, ids_s = scratch[:7]
    first_rows = scratch.pop()
    partz, sumz, partb, sendz, recvz, sendb, recvb = scratch[-7:]
    scratch = scratch[:-7]
    parts, weight, crossed, mixed, total_ref = scratch[7:12]
    gram, part0, sum0, part1, sum1, part2, share, full, window_ref = scratch[12:21]
    z_send, z_recv, p_send, p_recv, l_sem, i_send, i_recv, x_send, x_recv = scratch[21:30]
    q_send, q_recv, relayed, y_recv, y_send = scratch[30:35]
    send0, recv0, send1, recv1, send2, recv2, send3, recv3 = scratch[35:]
    width = count * tile // blocks
    total = rows * chips
    owners = rows * OWNERS
    row = lax.axis_index("row")
    orb = lax.axis_index("orb")
    chip = orb // CORES
    core = orb % CORES
    row_peers = [(lax.rem(row + t, rows), orb) for t in range(1, rows)]
    partner = (row, chip * CORES + 1 - core)
    me = row * chips + chip
    side_of = chip // 2
    mate = chip + 1 - 2 * (chip % 2)
    owner = (chip > 0) & (chip < chips - 1)
    home = row * OWNERS + side_of

    def place(k):
        other = lax.rem(me + k, total)
        return (other // chips, lax.rem(other, chips) * CORES + core)

    greet([place(k) for k in range(1, total)] + [partner])

    window = pltpu.make_async_copy(
        coef_ref.at[:, pl.ds(0, window_ref.shape[1])], window_ref, l_sem.at[4]
    )

    def z_copy(route, h, device):
        return remote(
            first_rows.at[h] if routes[route][0] == 1 else raw[route - 2, h],
            raw[route, h],
            z_send.at[route, h],
            z_recv.at[route, h],
            device,
        )

    def inside(where):
        return (where >= 0) & (where < chips)

    def towards(route, h):
        d, s = routes[route]
        there = chip + s
        valid = inside(there) & inside(chip - s * (d - 1))
        if d == 1 and h == SPLIT - 1:
            valid = valid & inside(there + s)
        return there, valid

    def origin(route):
        d, s = routes[route]
        there = chip - s * d
        return there, inside(there)

    tiles = own.shape[0]

    def every(source_rows, target, sem, act):
        step = 8

        def some(index, carry):
            for n in range(step):
                which = index * step + n
                at = pl.ds(pl.multiple_of(which * tile, tile), tile)
                act(pltpu.make_async_copy(coef_ref.at[source_rows, at], target.at[which], sem))
            return carry

        lax.fori_loop(0, tiles // step, some, 0)

    def first_piece(h, act):
        start = pl.multiple_of(h * group + row * piece, piece)
        every(pl.ds(start, piece), first_rows.at[h], l_sem.at[5 + h], act)

    all_rows = pl.ds(0, orb_local)
    for h in range(SPLIT):
        first_piece(h, lambda copy: copy.start())
    bring = pltpu.make_async_copy(ints_ref, both.at[0], l_sem.at[2])
    swap = remote(ints_ref, both.at[1], i_send.at[0], i_recv.at[0], partner)
    for h in range(SPLIT):
        first_piece(h, lambda copy: copy.wait())
        for route in range(2):
            there, valid = towards(route, h)

            @pl.when(valid)
            def _():
                z_copy(route, h, (row, there * CORES + core)).start()

    every(all_rows, own, l_sem.at[0], lambda copy: copy.start())
    bring.start()
    swap.start()
    id_copies = []
    for t in range(1, rows):
        id_copies.append(
            remote(ids_ref, ids_v.at[t], i_send.at[t], i_recv.at[t], row_peers[t - 1])
        )
        id_copies[-1].start()

    window.start()
    first = pltpu.make_async_copy(ids_ref, ids_s.at[0], l_sem.at[1])
    first.start()
    first.wait()
    for t in range(1, rows):
        id_copies[t - 1].wait()
        move = pltpu.make_async_copy(ids_v.at[t], ids_s.at[t], l_sem.at[1])
        move.start()
        move.wait()

    def take(source, targets, t):
        step = 8

        def some(block, carry):
            for k in range(step):
                slot = block * step + k
                at = pl.ds(pl.multiple_of(slot * tile, tile), tile)
                value = source[ids_s[t, 0, slot]]
                height = value.shape[0] // len(targets)
                for n, target in enumerate(targets):
                    target[:, at] = value[n * height : (n + 1) * height]
            return carry

        lax.fori_loop(0, count // step, some, 0)

    def band(from_row):
        return pl.ds(pl.multiple_of(from_row * piece, piece), piece)

    def spread(from_row, came, h, t, device):
        k = lax.rem(came + chips - chip, chips) - 1
        return remote(
            staged.at[k, h, t - 1],
            kept.at[came, h, band(from_row), :],
            p_send.at[k, h, t],
            p_recv.at[k, h, t],
            device,
        )

    direct = remote(
        kept.at[chip, SPLIT - 1],
        kept.at[chip, SPLIT - 1],
        q_send,
        q_recv,
        (row, mate * CORES + core),
    )

    whole = pl.ds(0, CORES * aux_local)

    def handout(came, h, k, some=whole):
        to = lax.rem(home + k, owners)
        return remote(
            ready.at[came, h, to, some],
            parts.at[came, h, row, chip, some],
            x_send.at[came, h, k],
            x_recv.at[came, h, me],
            (to // OWNERS, (1 + lax.rem(to, OWNERS)) * CORES + core),
        )

    def keep(came, h, some=whole):
        return pltpu.make_async_copy(
            ready.at[came, h, home, some],
            parts.at[came, h, row, chip, some],
            x_send.at[came, h, 0],
        )

    def along(came, h, side, some=whole):
        return remote(
            ready.at[came, h, row * OWNERS + side, some],
            parts.at[came, h, row, chip, some],
            x_send.at[came, h, side],
            x_recv.at[came, h, me],
            (row, (1 + side) * CORES + core),
        )

    def across(came, h, t, some=whole):
        to = lax.rem(row + t, rows)
        return remote(
            ready.at[came, h, pl.ds(to * OWNERS, OWNERS), some],
            relayed.at[came, h, t - 1, :, some],
            x_send.at[came, h, OWNERS + t],
            y_recv.at[came, h, t - 1],
            (to, orb),
        )

    def onwards(came, h, t, side):
        source = lax.rem(row + rows - t, rows)
        return remote(
            relayed.at[came, h, t - 1, side],
            parts.at[came, h, source, chip],
            y_send.at[came, h, t - 1, side],
            x_recv.at[came, h, source * chips + chip],
            (row, (1 + side) * CORES + core),
        )

    def hand(came, h, some=whole):
        @pl.when(owner)
        def _():
            keep(came, h, some).start()
            for k in range(1, owners):
                handout(came, h, k, some).start()

        @pl.when(jnp.logical_not(owner))
        def _():
            for t in range(1, rows):
                across(came, h, t, some).start()
            for side in range(OWNERS):
                along(came, h, side, some).start()

    def forward(came, h):
        for t in range(1, rows):
            across(came, h, t).wait_recv()
            for side in range(OWNERS):
                onwards(came, h, t, side).start()

    def slot_of(side):
        return (core + side - 2 * core * side) * aux_local

    def some_products(lhs_of, side, block, store):
        lhs = lhs_of(pl.ds(pl.multiple_of(block * width, width), width))
        at = pl.ds(pl.multiple_of(block * tile, tile), tile)
        rhs = both[side, :, at, :].reshape(aux_local * tile, width)
        result = lax.dot_general(
            lhs, rhs, (((1,), (1,)), ((), ())), preferred_element_type=jnp.float32
        )
        for p in range(aux_local):
            value = result[:, p * tile : (p + 1) * tile].astype(ready.dtype)
            store(slot_of(side) + p, at, value)

    def product(came, h):
        def one(step, carry):
            side = step // blocks

            def store(slot, at, value):
                ready[came, h, :, slot, :, at] = value.reshape(owners, part, tile)

            some_products(
                lambda at: kept[came, h, :, at], side, step - side * blocks, store
            )
            return carry

        lax.fori_loop(0, CORES * blocks, one, 0)

        hand(came, h)

    def own_product(side):
        def one(block, carry):
            def store(slot, at, value):
                for h in range(SPLIT):
                    rows_of_h = value[h * group : (h + 1) * group]
                    ready[chip, h, :, slot, :, at] = rows_of_h.reshape(owners, part, tile)

            some_products(
                lambda at: kept[chip, :, :, at].reshape(orb_local, width), side, block, store
            )
            return carry

        lax.fori_loop(0, blocks, one, 0)
        some = pl.ds(slot_of(side), aux_local)
        for h in range(SPLIT):
            hand(chip, h, some)

    every(all_rows, own, l_sem.at[0], lambda copy: copy.wait())
    take(own, [kept.at[chip, h] for h in range(SPLIT)], 0)

    @pl.when(jnp.logical_not(owner))
    def _():
        direct.start()

    def pass_on(d):
        for h in range(SPLIT):
            for route in range(len(routes)):
                if routes[route][0] != d:
                    continue
                s = routes[route][1]
                came, valid = origin(route)
                special = d == 1 and h == SPLIT - 1

                @pl.when(valid & inside(chip + s) if special else valid)
                def _():
                    z_copy(route, h, partner).wait_recv()
                    if d + 1 < chips:
                        there, onward = towards(route + 2, h)

                        @pl.when(onward)
                        def _():
                            z_copy(route + 2, h, (row, there * CORES + core)).start()

                @pl.when(valid & (came != mate) if special else valid)
                def _():
                    k = lax.rem(came + chips - chip, chips) - 1
                    for t in range(1, rows):
                        take(raw[route, h], [staged.at[k, h, t - 1]], t)
                        spread(row, came, h, t, row_peers[rows - t - 1]).start()
                    take(raw[route, h], [kept.at[came, h, band(row), :]], 0)

    def multiply(d, pieces=range(SPLIT)):
        for h in pieces:
            for route in range(len(routes)):
                if routes[route][0] != d:
                    continue
                came, valid = origin(route)
                special = d == 1 and h == SPLIT - 1

                @pl.when(valid & (came != mate) if special else valid)
                def _():
                    for t in range(1, rows):
                        source_row = lax.rem(row + t, rows)
                        spread(source_row, came, h, t, row_peers[0]).wait_recv()
                    product(came, h)

    def multiply_direct():
        remote(
            kept.at[mate, SPLIT - 1], kept.at[mate, SPLIT - 1], q_send, q_recv, partner
        ).wait_recv()
        product(mate, SPLIT - 1)

    def prepare():
        height = weight.shape[1]
        aux = metric_ref.shape[0]
        at = lax.broadcasted_iota(jnp.int32, (height, aux), 0)
        which = lax.broadcasted_iota(jnp.int32, (height, aux), 1)
        expand = jnp.where(at // part == which, 1.0, 0.0).astype(jnp.float32)
        left = lax.dot_general(
            expand,
            metric_ref[...],
            (((1,), (1,)), ((), ())),
            precision=lax.Precision.HIGHEST,
            preferred_element_type=jnp.float32,
        )
        wide = lax.dot_general(
            left,
            expand,
            (((1,), (1,)), ((), ())),
            precision=lax.Precision.HIGHEST,
            preferred_element_type=jnp.float32,
        )
        a = lax.broadcasted_iota(jnp.int32, (height, height), 0)
        b = lax.broadcasted_iota(jnp.int32, (height, height), 1)
        wide = jnp.where(a % part == b % part, wide, 0.0)
        high = wide.astype(weight.dtype)
        weight[0] = high
        weight[1] = (wide - high.astype(jnp.float32)).astype(weight.dtype)
        for r in range(rows):
            total_ref[r] = jnp.zeros(total_ref.shape[1:], jnp.float32)

    bring.wait()
    own_product(0)
    pass_on(1)
    swap.wait()
    own_product(1)
    pass_on(2)

    @pl.when(owner)
    def _():
        direct.start()
        prepare()

    multiply(1)

    @pl.when(owner)
    def _():
        multiply_direct()

    pass_on(3)
    end = jnp.logical_not(owner)
    inward = 1 - 2 * side_of

    @pl.when(end)
    def _():
        for h in range(SPLIT):
            forward(chip, h)
        forward(mate, 0)

    multiply(2)
    multiply(3, [0])

    @pl.when(end)
    def _():
        for h in range(SPLIT):
            forward(chip + 2 * inward, h)
        multiply_direct()
        forward(chip + 3 * inward, 0)

    multiply(3, [1])

    @pl.when(end)
    def _():
        forward(mate, SPLIT - 1)
        forward(chip + 3 * inward, SPLIT - 1)

    def collect(came, h):
        def arrive(k, carry):
            source = lax.rem(me + k, total)
            remote(
                ready.at[came, h, 0],
                parts.at[came, h, source // chips, lax.rem(source, chips)],
                x_send.at[came, h, 0],
                x_recv.at[came, h, source],
                partner,
            ).wait_recv()
            return carry

        lax.fori_loop(1, total, arrive, 0)
        keep(came, h).wait()
        height = weight.shape[1]
        local = mixed.shape[2]
        for r in range(rows):
            value = parts[came, h, r].astype(jnp.float32).reshape(height, local)
            value = value.astype(mixed.dtype)
            result = jnp.dot(weight[0], value, preferred_element_type=jnp.float32)
            result = result + jnp.dot(weight[1], value, preferred_element_type=jnp.float32)
            mixed[r] = result.astype(mixed.dtype)
            crossed[r * local : (r + 1) * local, :] = value.T

        def add(r, carry):
            total_ref[r] += jnp.dot(
                crossed[...], mixed[r], preferred_element_type=jnp.float32
            )
            return carry

        lax.fori_loop(0, rows, add, 0)

    height = share.shape[0]
    half = height * OWNERS
    quarter = height // 2
    first_copies, second_copies, last_copies = [], [], []
    across_copies, after_copies = [], []
    order = [lax.rem(row + t, rows) for t in range(1, rows)] + [row]
    near = 1 + side_of
    far = OWNERS - side_of
    for t, peer in enumerate(order):
        first_copies.append(
            remote(gram.at[peer], part0.at[peer], send0.at[t], recv0.at[t], partner)
        )
        start = pl.multiple_of((1 - side_of) * height + quarter, quarter)
        across_copies.append(
            remote(
                sum0.at[peer, pl.ds(start, quarter)],
                partz.at[peer],
                sendz.at[t],
                recvz.at[t],
                (row, far * CORES + core),
            )
        )
        if t < rows - 1:
            second_copies.append(
                [
                    remote(
                        sum0.at[peer, pl.ds(side * height, quarter)],
                        part1.at[t, side],
                        send1.at[t, side],
                        recv1.at[t, side],
                        (peer, orb),
                    )
                    for side in range(OWNERS)
                ]
            )
            after_copies.append(
                remote(sumz.at[peer], partb.at[t], sendb.at[t], recvb.at[t], (peer, orb))
            )
    third = remote(
        sum1.at[1 - side_of], part2, send2, recv2, (row, far * CORES + core)
    )

    def block(from_core, from_side):
        start = pl.multiple_of(from_core * half + from_side * height, height)
        return full.at[pl.ds(start, height), :]

    own_block = block(core, side_of)
    targets = [
        ((row, far * CORES + core), 0),
        ((row, mate * CORES + core), 0),
        ((row, (chips - 1 - mate) * CORES + core), 0),
        (partner, 1),
    ]
    for n, (device, kind) in enumerate(targets):
        last_copies.append(
            remote(share, own_block, send3.at[n], recv3.at[kind, side_of], device)
        )

    def publish(which):
        at = which * quarter
        start = core * half + side_of * height + at
        target = full.at[pl.ds(pl.multiple_of(start, quarter), quarter), :]
        for n, (device, kind) in enumerate(targets):
            remote(
                share.at[pl.ds(at, quarter)],
                target,
                send3.at[n],
                recv3.at[kind, side_of],
                device,
            ).start()

    def relay(side, n):
        return remote(
            block(core, side), block(core, side), send3.at[n], recv3.at[1, side], partner
        )

    def landed(from_core, side, kind):
        remote(
            share, block(from_core, side), send3.at[0], recv3.at[kind, side], partner
        ).wait_recv()

    mine_half = pl.ds(pl.multiple_of(core * half, half), half)
    other_half = pl.ds(pl.multiple_of((1 - core) * half, half), half)

    @pl.when(owner)
    def _():
        def inner(u, carry):
            collect(1 + lax.rem(u, 2), u // 2)
            return carry

        def outer(u, carry):
            collect((chips - 1) * lax.rem(u, 2), u // 2)
            return carry

        for h in range(SPLIT):
            lax.fori_loop(h * OWNERS, (h + 1) * OWNERS, inner, 0)
            lax.fori_loop(h * OWNERS, (h + 1) * OWNERS, outer, 0)
        for t, peer in enumerate(order):
            gram[peer] = total_ref[peer, other_half].astype(gram.dtype)
            first_copies[t].start()
        for t, peer in enumerate(order):
            first_copies[t].wait_recv()
            value = total_ref[peer, mine_half] + part0[peer].astype(jnp.float32)
            sum0[peer] = value.astype(sum0.dtype)
            across_copies[t].start()
            if t < rows - 1:
                for copy in second_copies[t]:
                    copy.start()
        for t, peer in enumerate(order):
            across_copies[t].wait_recv()
            start = pl.multiple_of(side_of * height + quarter, quarter)
            value = sum0[peer, pl.ds(start, quarter)].astype(jnp.float32)
            sumz[peer] = (value + partz[peer].astype(jnp.float32)).astype(sumz.dtype)
            if t < rows - 1:
                after_copies[t].start()
        for copies in second_copies:
            for copy in copies:
                copy.wait_recv()
        for side in range(OWNERS):
            value = sum0[row, side * height : side * height + quarter].astype(jnp.float32)
            for t in range(rows - 1):
                value = value + part1[t, side].astype(jnp.float32)
            sum1[side] = value.astype(sum1.dtype)
        third.start()
        for copy in after_copies:
            copy.wait_recv()
        value = sumz[row].astype(jnp.float32)
        for t in range(rows - 1):
            value = value + partb[t].astype(jnp.float32)
        share[quarter:] = value.astype(share.dtype)
        publish(1)
        third.wait_recv()
        value = sum1[side_of].astype(jnp.float32) + part2[...].astype(jnp.float32)
        share[:quarter] = value.astype(share.dtype)
        publish(0)
        start = pl.multiple_of(core * half + side_of * height, height)
        full[pl.ds(start, height), :] = share[...]
        landed(core, 1 - side_of, 0)
        relay(1 - side_of, 4).start()

    @pl.when(jnp.logical_not(owner))
    def _():
        landed(core, side_of, 0)
        relay(side_of, 4).start()
        landed(core, 1 - side_of, 0)
        relay(1 - side_of, 5).start()

    window.wait()
    result = jnp.dot(
        window_ref[:, mine_half], full[mine_half, :], preferred_element_type=jnp.float32
    )
    for side in range(OWNERS):
        landed(1 - core, side, 1)
    out_ref[...] = result + jnp.dot(
        window_ref[:, other_half], full[other_half, :], preferred_element_type=jnp.float32
    )

    @pl.when(owner)
    def _():
        for copy in sum(second_copies, first_copies + across_copies + after_copies):
            copy.wait_send()
        for copy in [third] + last_copies:
            copy.wait_send()
        relay(1 - side_of, 4).wait_send()

    @pl.when(jnp.logical_not(owner))
    def _():
        relay(side_of, 4).wait_send()
        relay(1 - side_of, 5).wait_send()

    direct.wait_send()
    for route in range(len(routes)):
        d = routes[route][0]
        came, valid = origin(route)
        for h in range(SPLIT):
            there, sent = towards(route, h)
            special = d == 1 and h == SPLIT - 1

            @pl.when(sent)
            def _():
                z_copy(route, h, (row, there * CORES + core)).wait_send()

            @pl.when(valid & (came != mate) if special else valid)
            def _():
                for t in range(1, rows):
                    spread(row, came, h, t, row_peers[rows - t - 1]).wait_send()

    for came in range(chips):
        for h in range(SPLIT):

            @pl.when(owner)
            def _():
                for k in range(1, owners):
                    handout(came, h, k).wait_send()

            @pl.when(jnp.logical_not(owner))
            def _():
                for side in range(OWNERS):
                    along(came, h, side).wait_send()
                for t in range(1, rows):
                    across(came, h, t).wait_send()
                    for side in range(OWNERS):
                        onwards(came, h, t, side).wait_send()


def exchange(integrals, ids, coefficients, metric, rows, orbs, blocks, count):
    chips = orbs // CORES
    orb_local, basis = coefficients.shape
    aux_local, local_rows, _ = integrals.shape
    tile = local_rows // blocks
    owners = rows * OWNERS
    piece = orb_local // rows // SPLIT
    group = piece * rows
    part = group // owners
    aux = aux_local * orbs
    window = local_rows * rows
    half = window // CORES
    height = half // OWNERS
    quarter = height // 2
    routes = 2 * (chips - 1)
    dtype = coefficients.dtype
    scratch = [
        pltpu.VMEM((basis // tile, piece, tile), dtype) for _ in range(routes * SPLIT)
    ]
    scratch += [
        pltpu.VMEM((basis // tile, orb_local, tile), dtype),
        pltpu.VMEM((chips, SPLIT, group, count * tile), dtype),
        pltpu.VMEM((chips - 1, SPLIT, rows - 1, piece, count * tile), dtype),
        pltpu.VMEM((CORES,) + integrals.shape, dtype),
        pltpu.VMEM((chips, SPLIT, owners, CORES * aux_local, part, local_rows), dtype),
        pltpu.VMEM((rows, 1, ids.shape[1]), jnp.int32),
        pltpu.SMEM((rows, 1, ids.shape[1]), jnp.int32),
        pltpu.VMEM((chips, SPLIT, rows, chips, CORES * aux_local, part, local_rows), dtype),
        pltpu.VMEM((2, aux * part, aux * part), dtype),
        pltpu.VMEM((window, aux * part), dtype),
        pltpu.VMEM((rows, aux * part, local_rows), dtype),
        pltpu.VMEM((rows, window, local_rows), jnp.float32),
        pltpu.VMEM((rows, half, local_rows), dtype),
        pltpu.VMEM((rows, half, local_rows), dtype),
        pltpu.VMEM((rows, half, local_rows), dtype),
        pltpu.VMEM((rows - 1, OWNERS, quarter, local_rows), dtype),
        pltpu.VMEM((OWNERS, quarter, local_rows), dtype),
        pltpu.VMEM((quarter, local_rows), dtype),
        pltpu.VMEM((height, local_rows), dtype),
        pltpu.VMEM((window, local_rows), dtype),
        pltpu.VMEM((orb_local, window), dtype),
        pltpu.SemaphoreType.DMA((routes, SPLIT)),
        pltpu.SemaphoreType.DMA((routes, SPLIT)),
        pltpu.SemaphoreType.DMA((chips - 1, SPLIT, rows)),
        pltpu.SemaphoreType.DMA((chips - 1, SPLIT, rows)),
        pltpu.SemaphoreType.DMA((5 + SPLIT,)),
        pltpu.SemaphoreType.DMA((rows,)),
        pltpu.SemaphoreType.DMA((rows,)),
        pltpu.SemaphoreType.DMA((chips, SPLIT, owners)),
        pltpu.SemaphoreType.DMA((chips, SPLIT, rows * chips)),
        pltpu.SemaphoreType.DMA,
        pltpu.SemaphoreType.DMA,
        pltpu.VMEM(
            (chips, SPLIT, rows - 1, OWNERS, CORES * aux_local, part, local_rows), dtype
        ),
        pltpu.SemaphoreType.DMA((chips, SPLIT, rows - 1)),
        pltpu.SemaphoreType.DMA((chips, SPLIT, rows - 1, OWNERS)),
        pltpu.SemaphoreType.DMA((rows,)),
        pltpu.SemaphoreType.DMA((rows,)),
        pltpu.SemaphoreType.DMA((rows, OWNERS)),
        pltpu.SemaphoreType.DMA((rows, OWNERS)),
        pltpu.SemaphoreType.DMA,
        pltpu.SemaphoreType.DMA,
        pltpu.SemaphoreType.DMA((6,)),
        pltpu.SemaphoreType.DMA((2, OWNERS)),
        pltpu.VMEM((rows, quarter, local_rows), dtype),
        pltpu.VMEM((rows, quarter, local_rows), dtype),
        pltpu.VMEM((rows - 1, quarter, local_rows), dtype),
        pltpu.SemaphoreType.DMA((rows,)),
        pltpu.SemaphoreType.DMA((rows,)),
        pltpu.SemaphoreType.DMA((rows,)),
        pltpu.SemaphoreType.DMA((rows,)),
        pltpu.VMEM((SPLIT, basis // tile, piece, tile), dtype),
    ]
    dims = (rows, chips, orb_local, tile, count, aux_local, blocks, part)
    return pl.pallas_call(
        functools.partial(exchange_kernel, dims),
        out_shape=jax.ShapeDtypeStruct((orb_local, local_rows), jnp.float32),
        in_specs=[pl.BlockSpec(memory_space=pltpu.VMEM)] * 2
        + [pl.BlockSpec(memory_space=pl.ANY)] * 2,
        out_specs=pl.BlockSpec(memory_space=pltpu.VMEM),
        scratch_shapes=scratch,
        compiler_params=pltpu.CompilerParams(
            collective_id=0, has_side_effects=True, vmem_limit_bytes=63 << 20
        ),
    )(ids, metric, coefficients, integrals)


def per_device(rows, orbs, integrals, tile_ids, coefficients, metric):
    orb_local, basis_width = coefficients.shape
    block_count, kept_count = tile_ids.shape
    chips = orbs // CORES
    if (
        chips != 2 * OWNERS
        or orb_local % (16 * SPLIT * rows)
        or orb_local % (8 * SPLIT * OWNERS * rows)
        or block_count * kept_count % 8
        or basis_width // (integrals.shape[1] // block_count) % 8
    ):
        return plain_device(rows, orbs, integrals, tile_ids, coefficients, metric)
    count = block_count * kept_count
    lanes = -(-count // 128) * 128
    ids = jnp.pad(tile_ids.reshape(1, count), ((0, 0), (0, lanes - count)))
    return exchange(integrals, ids, coefficients, metric, rows, orbs, block_count, count)


def plain_device(rows, orbs, integrals, tile_ids, coefficients, metric):
    aux_local, local_rows, kept_width = integrals.shape
    orb_local, basis_width = coefficients.shape
    block_count, kept_count = tile_ids.shape
    tile_rows = local_rows // block_count
    orbitals = orb_local * orbs
    aux = aux_local * orbs
    window = local_rows * rows
    part = orbitals // (rows * orbs)
    picked = pick(coefficients, tile_ids.reshape(block_count * kept_count), tile_rows)
    col_piece = lax.all_gather(picked, "orb", axis=0, tiled=True)
    slabs = integrals.reshape(aux_local, block_count, tile_rows, kept_width)
    halves = [
        jnp.einsum(
            "pmk,jk->pjm",
            slabs[:, b],
            col_piece[:, b * kept_width : (b + 1) * kept_width],
            preferred_element_type=jnp.float32,
        ).astype(jnp.bfloat16)
        for b in range(block_count)
    ]
    halves = jnp.concatenate(halves, axis=2)
    outgoing = halves.reshape(aux_local, rows * orbs, part, local_rows).transpose(1, 0, 2, 3)
    by_part = lax.all_to_all(outgoing, ("row", "orb"), split_axis=0, concat_axis=0, tiled=True)
    by_part = by_part.reshape(rows, aux, part, local_rows)
    mixed = jnp.einsum(
        "pq,rpjm->rqjm", metric, by_part.astype(jnp.float32), precision=lax.Precision.HIGHEST
    ).astype(jnp.bfloat16)
    gram = jnp.einsum(
        "rqjm,sqjn->rmsn", by_part, mixed, preferred_element_type=jnp.float32
    ).astype(jnp.bfloat16)
    gram = gram.reshape(orbs, window // orbs, rows, local_rows).transpose(2, 0, 1, 3)
    gram = gram.reshape(rows * window, local_rows)
    share = lax.psum_scatter(gram, ("row", "orb"), scatter_dimension=0, tiled=True)
    columns = lax.all_gather(share, "orb", axis=0, tiled=True)
    return jnp.dot(coefficients[:, :window], columns, preferred_element_type=jnp.float32)


def solution(mesh):
    return jax.shard_map(
        functools.partial(per_device, mesh.shape["row"], mesh.shape["orb"]),
        mesh=mesh,
        in_specs=(P("orb", "row", None), P("row", None), P("orb", None), P()),
        out_specs=P("orb", "row"),
        check_vma=False,
    )
```

```python
import functools

import jax
import jax.numpy as jnp
from jax import lax
from jax.experimental import pallas as pl
from jax.experimental.pallas import tpu as pltpu
from jax.sharding import PartitionSpec as P


def pick_kernel(count, tile, ids_ref, coef_ref, out_ref, sem):
    def begin(slot, carry):
        source = pl.ds(pl.multiple_of(ids_ref[slot] * tile, tile), tile)
        target = pl.ds(pl.multiple_of(slot * tile, tile), tile)
        pltpu.make_async_copy(coef_ref.at[:, source], out_ref.at[:, target], sem).start()
        return carry

    lax.fori_loop(0, count, begin, 0)
    pltpu.make_async_copy(coef_ref.at[:, pl.ds(0, count * tile)], out_ref, sem).wait()


def pick(coefficients, ids, tile):
    count = ids.shape[0]
    return pl.pallas_call(
        functools.partial(pick_kernel, count, tile),
        out_shape=jax.ShapeDtypeStruct((coefficients.shape[0], count * tile), coefficients.dtype),
        in_specs=[
            pl.BlockSpec(memory_space=pltpu.SMEM),
            pl.BlockSpec(memory_space=pl.ANY),
        ],
        out_specs=pl.BlockSpec(memory_space=pltpu.VMEM),
        scratch_shapes=[pltpu.SemaphoreType.DMA],
    )(ids, coefficients)


MESH = pl.DeviceIdType.MESH
CORES = 2
SPLIT = 2
OWNERS = 2


def greet(peers):
    barrier = pltpu.get_barrier_semaphore()
    for peer in peers:
        pl.semaphore_signal(barrier, inc=1, device_id=peer, device_id_type=MESH)
    pl.semaphore_wait(barrier, len(peers))


def remote(source, target, send, recv, device):
    return pltpu.make_async_remote_copy(
        src_ref=source,
        dst_ref=target,
        send_sem=send,
        recv_sem=recv,
        device_id=device,
        device_id_type=MESH,
    )


def exchange_kernel(dims, ids_ref, metric_ref, coef_ref, ints_ref, out_ref, *scratch):
    rows, chips, orb_local, tile, count, aux_local, blocks, part = dims
    piece = orb_local // rows // SPLIT
    group = piece * rows
    routes = [(d, s) for d in range(1, chips) for s in (1, -1)]
    scratch = list(scratch)
    raw = {}
    for route in range(len(routes)):
        for h in range(SPLIT):
            raw[route, h] = scratch.pop(0)
    own, kept, staged, both, ready, ids_v, ids_s = scratch[:7]
    first_rows = scratch.pop()
    partz, sumz, partb, sendz, recvz, sendb, recvb = scratch[-7:]
    scratch = scratch[:-7]
    parts, weight, crossed, mixed, total_ref = scratch[7:12]
    gram, part0, sum0, part1, sum1, part2, share, full, window_ref = scratch[12:21]
    z_send, z_recv, p_send, p_recv, l_sem, i_send, i_recv, x_send, x_recv = scratch[21:30]
    q_send, q_recv, relayed, y_recv, y_send = scratch[30:35]
    send0, recv0, send1, recv1, send2, recv2, send3, recv3 = scratch[35:]
    width = count * tile // blocks
    total = rows * chips
    owners = rows * OWNERS
    row = lax.axis_index("row")
    orb = lax.axis_index("orb")
    chip = orb // CORES
    core = orb % CORES
    row_peers = [(lax.rem(row + t, rows), orb) for t in range(1, rows)]
    partner = (row, chip * CORES + 1 - core)
    me = row * chips + chip
    side_of = chip // 2
    mate = chip + 1 - 2 * (chip % 2)
    owner = (chip > 0) & (chip < chips - 1)
    home = row * OWNERS + side_of

    def place(k):
        other = lax.rem(me + k, total)
        return (other // chips, lax.rem(other, chips) * CORES + core)

    greet([place(k) for k in range(1, total)] + [partner])

    window = pltpu.make_async_copy(
        coef_ref.at[:, pl.ds(0, window_ref.shape[1])], window_ref, l_sem.at[4]
    )

    def z_copy(route, h, device):
        return remote(
            first_rows.at[h] if routes[route][0] == 1 else raw[route - 2, h],
            raw[route, h],
            z_send.at[route, h],
            z_recv.at[route, h],
            device,
        )

    def inside(where):
        return (where >= 0) & (where < chips)

    def towards(route, h):
        d, s = routes[route]
        there = chip + s
        valid = inside(there) & inside(chip - s * (d - 1))
        if d == 1 and h == SPLIT - 1:
            valid = valid & inside(there + s)
        return there, valid

    def origin(route):
        d, s = routes[route]
        there = chip - s * d
        return there, inside(there)

    tiles = own.shape[0]

    def every(source_rows, target, sem, act):
        step = 8

        def some(index, carry):
            for n in range(step):
                which = index * step + n
                at = pl.ds(pl.multiple_of(which * tile, tile), tile)
                act(pltpu.make_async_copy(coef_ref.at[source_rows, at], target.at[which], sem))
            return carry

        lax.fori_loop(0, tiles // step, some, 0)

    def first_piece(h, act):
        start = pl.multiple_of(h * group + row * piece, piece)
        every(pl.ds(start, piece), first_rows.at[h], l_sem.at[5 + h], act)

    all_rows = pl.ds(0, orb_local)
    for h in range(SPLIT):
        first_piece(h, lambda copy: copy.start())
    bring = pltpu.make_async_copy(ints_ref, both.at[0], l_sem.at[2])
    swap = remote(ints_ref, both.at[1], i_send.at[0], i_recv.at[0], partner)
    for h in range(SPLIT):
        first_piece(h, lambda copy: copy.wait())
        for route in range(2):
            there, valid = towards(route, h)

            @pl.when(valid)
            def _():
                z_copy(route, h, (row, there * CORES + core)).start()

    every(all_rows, own, l_sem.at[0], lambda copy: copy.start())
    bring.start()
    swap.start()
    id_copies = []
    for t in range(1, rows):
        id_copies.append(
            remote(ids_ref, ids_v.at[t], i_send.at[t], i_recv.at[t], row_peers[t - 1])
        )
        id_copies[-1].start()

    window.start()
    first = pltpu.make_async_copy(ids_ref, ids_s.at[0], l_sem.at[1])
    first.start()
    first.wait()
    for t in range(1, rows):
        id_copies[t - 1].wait()
        move = pltpu.make_async_copy(ids_v.at[t], ids_s.at[t], l_sem.at[1])
        move.start()
        move.wait()

    def take(source, targets, t):
        step = 8

        def some(block, carry):
            for k in range(step):
                slot = block * step + k
                at = pl.ds(pl.multiple_of(slot * tile, tile), tile)
                value = source[ids_s[t, 0, slot]]
                height = value.shape[0] // len(targets)
                for n, target in enumerate(targets):
                    target[:, at] = value[n * height : (n + 1) * height]
            return carry

        lax.fori_loop(0, count // step, some, 0)

    def band(from_row):
        return pl.ds(pl.multiple_of(from_row * piece, piece), piece)

    def spread(from_row, came, h, t, device):
        k = lax.rem(came + chips - chip, chips) - 1
        return remote(
            staged.at[k, h, t - 1],
            kept.at[came, h, band(from_row), :],
            p_send.at[k, h, t],
            p_recv.at[k, h, t],
            device,
        )

    direct = remote(
        kept.at[chip, SPLIT - 1],
        kept.at[chip, SPLIT - 1],
        q_send,
        q_recv,
        (row, mate * CORES + core),
    )

    whole = pl.ds(0, CORES * aux_local)

    def handout(came, h, k, some=whole):
        to = lax.rem(home + k, owners)
        return remote(
            ready.at[came, h, to, some],
            parts.at[came, h, row, chip, some],
            x_send.at[came, h, k],
            x_recv.at[came, h, me],
            (to // OWNERS, (1 + lax.rem(to, OWNERS)) * CORES + core),
        )

    def keep(came, h, some=whole):
        return pltpu.make_async_copy(
            ready.at[came, h, home, some],
            parts.at[came, h, row, chip, some],
            x_send.at[came, h, 0],
        )

    def along(came, h, side, some=whole):
        return remote(
            ready.at[came, h, row * OWNERS + side, some],
            parts.at[came, h, row, chip, some],
            x_send.at[came, h, side],
            x_recv.at[came, h, me],
            (row, (1 + side) * CORES + core),
        )

    def across(came, h, t, some=whole):
        to = lax.rem(row + t, rows)
        return remote(
            ready.at[came, h, pl.ds(to * OWNERS, OWNERS), some],
            relayed.at[came, h, t - 1, :, some],
            x_send.at[came, h, OWNERS + t],
            y_recv.at[came, h, t - 1],
            (to, orb),
        )

    def onwards(came, h, t, side):
        source = lax.rem(row + rows - t, rows)
        return remote(
            relayed.at[came, h, t - 1, side],
            parts.at[came, h, source, chip],
            y_send.at[came, h, t - 1, side],
            x_recv.at[came, h, source * chips + chip],
            (row, (1 + side) * CORES + core),
        )

    def hand(came, h, some=whole):
        @pl.when(owner)
        def _():
            keep(came, h, some).start()
            for k in range(1, owners):
                handout(came, h, k, some).start()

        @pl.when(jnp.logical_not(owner))
        def _():
            for t in range(1, rows):
                across(came, h, t, some).start()
            for side in range(OWNERS):
                along(came, h, side, some).start()

    def forward(came, h):
        for t in range(1, rows):
            across(came, h, t).wait_recv()
            for side in range(OWNERS):
                onwards(came, h, t, side).start()

    def slot_of(side):
        return (core + side - 2 * core * side) * aux_local

    def some_products(lhs_of, side, block, store):
        lhs = lhs_of(pl.ds(pl.multiple_of(block * width, width), width))
        at = pl.ds(pl.multiple_of(block * tile, tile), tile)
        rhs = both[side, :, at, :].reshape(aux_local * tile, width)
        result = lax.dot_general(
            lhs, rhs, (((1,), (1,)), ((), ())), preferred_element_type=jnp.float32
        )
        for p in range(aux_local):
            value = result[:, p * tile : (p + 1) * tile].astype(ready.dtype)
            store(slot_of(side) + p, at, value)

    def product(came, h):
        def one(step, carry):
            side = step // blocks

            def store(slot, at, value):
                ready[came, h, :, slot, :, at] = value.reshape(owners, part, tile)

            some_products(
                lambda at: kept[came, h, :, at], side, step - side * blocks, store
            )
            return carry

        lax.fori_loop(0, CORES * blocks, one, 0)

        hand(came, h)

    def own_product(side):
        def one(block, carry):
            def store(slot, at, value):
                for h in range(SPLIT):
                    rows_of_h = value[h * group : (h + 1) * group]
                    ready[chip, h, :, slot, :, at] = rows_of_h.reshape(owners, part, tile)

            some_products(
                lambda at: kept[chip, :, :, at].reshape(orb_local, width), side, block, store
            )
            return carry

        lax.fori_loop(0, blocks, one, 0)
        some = pl.ds(slot_of(side), aux_local)
        for h in range(SPLIT):
            hand(chip, h, some)

    every(all_rows, own, l_sem.at[0], lambda copy: copy.wait())
    take(own, [kept.at[chip, h] for h in range(SPLIT)], 0)

    @pl.when(jnp.logical_not(owner))
    def _():
        direct.start()

    def pass_on(d):
        for h in range(SPLIT):
            for route in range(len(routes)):
                if routes[route][0] != d:
                    continue
                s = routes[route][1]
                came, valid = origin(route)
                special = d == 1 and h == SPLIT - 1

                @pl.when(valid & inside(chip + s) if special else valid)
                def _():
                    z_copy(route, h, partner).wait_recv()
                    if d + 1 < chips:
                        there, onward = towards(route + 2, h)

                        @pl.when(onward)
                        def _():
                            z_copy(route + 2, h, (row, there * CORES + core)).start()

                @pl.when(valid & (came != mate) if special else valid)
                def _():
                    k = lax.rem(came + chips - chip, chips) - 1
                    for t in range(1, rows):
                        take(raw[route, h], [staged.at[k, h, t - 1]], t)
                        spread(row, came, h, t, row_peers[rows - t - 1]).start()
                    take(raw[route, h], [kept.at[came, h, band(row), :]], 0)

    def multiply(d, pieces=range(SPLIT)):
        for h in pieces:
            for route in range(len(routes)):
                if routes[route][0] != d:
                    continue
                came, valid = origin(route)
                special = d == 1 and h == SPLIT - 1

                @pl.when(valid & (came != mate) if special else valid)
                def _():
                    for t in range(1, rows):
                        source_row = lax.rem(row + t, rows)
                        spread(source_row, came, h, t, row_peers[0]).wait_recv()
                    product(came, h)

    def multiply_direct():
        remote(
            kept.at[mate, SPLIT - 1], kept.at[mate, SPLIT - 1], q_send, q_recv, partner
        ).wait_recv()
        product(mate, SPLIT - 1)

    def prepare():
        height = weight.shape[1]
        aux = metric_ref.shape[0]
        at = lax.broadcasted_iota(jnp.int32, (height, aux), 0)
        which = lax.broadcasted_iota(jnp.int32, (height, aux), 1)
        expand = jnp.where(at // part == which, 1.0, 0.0).astype(jnp.float32)
        left = lax.dot_general(
            expand,
            metric_ref[...],
            (((1,), (1,)), ((), ())),
            precision=lax.Precision.HIGHEST,
            preferred_element_type=jnp.float32,
        )
        wide = lax.dot_general(
            left,
            expand,
            (((1,), (1,)), ((), ())),
            precision=lax.Precision.HIGHEST,
            preferred_element_type=jnp.float32,
        )
        a = lax.broadcasted_iota(jnp.int32, (height, height), 0)
        b = lax.broadcasted_iota(jnp.int32, (height, height), 1)
        wide = jnp.where(a % part == b % part, wide, 0.0)
        high = wide.astype(weight.dtype)
        weight[0] = high
        weight[1] = (wide - high.astype(jnp.float32)).astype(weight.dtype)
        for r in range(rows):
            total_ref[r] = jnp.zeros(total_ref.shape[1:], jnp.float32)

    bring.wait()
    own_product(0)
    pass_on(1)
    swap.wait()
    own_product(1)
    pass_on(2)

    @pl.when(owner)
    def _():
        direct.start()
        prepare()

    multiply(1)

    @pl.when(owner)
    def _():
        multiply_direct()

    pass_on(3)
    end = jnp.logical_not(owner)
    inward = 1 - 2 * side_of

    @pl.when(end)
    def _():
        for h in range(SPLIT):
            forward(chip, h)

    multiply(2, [0])

    @pl.when(end)
    def _():
        forward(mate, 0)

    multiply(2, [1])

    @pl.when(end)
    def _():
        forward(chip + 2 * inward, 0)

    multiply(3, [0])

    @pl.when(end)
    def _():
        forward(chip + 2 * inward, 1)
        multiply_direct()
        forward(chip + 3 * inward, 0)

    multiply(3, [1])

    @pl.when(end)
    def _():
        forward(mate, SPLIT - 1)
        forward(chip + 3 * inward, SPLIT - 1)

    def collect(came, h):
        def arrive(k, carry):
            source = lax.rem(me + k, total)
            remote(
                ready.at[came, h, 0],
                parts.at[came, h, source // chips, lax.rem(source, chips)],
                x_send.at[came, h, 0],
                x_recv.at[came, h, source],
                partner,
            ).wait_recv()
            return carry

        lax.fori_loop(1, total, arrive, 0)
        keep(came, h).wait()
        height = weight.shape[1]
        local = mixed.shape[2]
        for r in range(rows):
            value = parts[came, h, r].astype(jnp.float32).reshape(height, local)
            value = value.astype(mixed.dtype)
            result = jnp.dot(weight[0], value, preferred_element_type=jnp.float32)
            result = result + jnp.dot(weight[1], value, preferred_element_type=jnp.float32)
            mixed[r] = result.astype(mixed.dtype)
            crossed[r * local : (r + 1) * local, :] = value.T

        def add(r, carry):
            total_ref[r] += jnp.dot(
                crossed[...], mixed[r], preferred_element_type=jnp.float32
            )
            return carry

        lax.fori_loop(0, rows, add, 0)

    height = share.shape[0]
    half = height * OWNERS
    quarter = height // 2
    first_copies, second_copies, last_copies = [], [], []
    across_copies, after_copies = [], []
    order = [lax.rem(row + t, rows) for t in range(1, rows)] + [row]
    near = 1 + side_of
    far = OWNERS - side_of
    for t, peer in enumerate(order):
        first_copies.append(
            remote(gram.at[peer], part0.at[peer], send0.at[t], recv0.at[t], partner)
        )
        start = pl.multiple_of((1 - side_of) * height + quarter, quarter)
        across_copies.append(
            remote(
                sum0.at[peer, pl.ds(start, quarter)],
                partz.at[peer],
                sendz.at[t],
                recvz.at[t],
                (row, far * CORES + core),
            )
        )
        if t < rows - 1:
            second_copies.append(
                [
                    remote(
                        sum0.at[peer, pl.ds(side * height, quarter)],
                        part1.at[t, side],
                        send1.at[t, side],
                        recv1.at[t, side],
                        (peer, orb),
                    )
                    for side in range(OWNERS)
                ]
            )
            after_copies.append(
                remote(sumz.at[peer], partb.at[t], sendb.at[t], recvb.at[t], (peer, orb))
            )
    third = remote(
        sum1.at[1 - side_of], part2, send2, recv2, (row, far * CORES + core)
    )

    def block(from_core, from_side):
        start = pl.multiple_of(from_core * half + from_side * height, height)
        return full.at[pl.ds(start, height), :]

    own_block = block(core, side_of)
    targets = [
        ((row, far * CORES + core), 0),
        ((row, mate * CORES + core), 0),
        ((row, (chips - 1 - mate) * CORES + core), 0),
        (partner, 1),
    ]
    for n, (device, kind) in enumerate(targets):
        last_copies.append(
            remote(share, own_block, send3.at[n], recv3.at[kind, side_of], device)
        )

    def publish(which):
        at = which * quarter
        start = core * half + side_of * height + at
        target = full.at[pl.ds(pl.multiple_of(start, quarter), quarter), :]
        for n, (device, kind) in enumerate(targets):
            remote(
                share.at[pl.ds(at, quarter)],
                target,
                send3.at[n],
                recv3.at[kind, side_of],
                device,
            ).start()

    def relay(side, n):
        return remote(
            block(core, side), block(core, side), send3.at[n], recv3.at[1, side], partner
        )

    def landed(from_core, side, kind):
        remote(
            share, block(from_core, side), send3.at[0], recv3.at[kind, side], partner
        ).wait_recv()

    mine_half = pl.ds(pl.multiple_of(core * half, half), half)
    other_half = pl.ds(pl.multiple_of((1 - core) * half, half), half)

    @pl.when(owner)
    def _():
        def inner(u, carry):
            collect(1 + lax.rem(u, 2), u // 2)
            return carry

        def outer(u, carry):
            collect((chips - 1) * lax.rem(u, 2), u // 2)
            return carry

        for h in range(SPLIT):
            lax.fori_loop(h * OWNERS, (h + 1) * OWNERS, inner, 0)
            lax.fori_loop(h * OWNERS, (h + 1) * OWNERS, outer, 0)
        for t, peer in enumerate(order):
            gram[peer] = total_ref[peer, other_half].astype(gram.dtype)
            first_copies[t].start()
        for t, peer in enumerate(order):
            first_copies[t].wait_recv()
            value = total_ref[peer, mine_half] + part0[peer].astype(jnp.float32)
            sum0[peer] = value.astype(sum0.dtype)
            across_copies[t].start()
            if t < rows - 1:
                for copy in second_copies[t]:
                    copy.start()
        for t, peer in enumerate(order):
            across_copies[t].wait_recv()
            start = pl.multiple_of(side_of * height + quarter, quarter)
            value = sum0[peer, pl.ds(start, quarter)].astype(jnp.float32)
            sumz[peer] = (value + partz[peer].astype(jnp.float32)).astype(sumz.dtype)
            if t < rows - 1:
                after_copies[t].start()
        for copies in second_copies:
            for copy in copies:
                copy.wait_recv()
        for side in range(OWNERS):
            value = sum0[row, side * height : side * height + quarter].astype(jnp.float32)
            for t in range(rows - 1):
                value = value + part1[t, side].astype(jnp.float32)
            sum1[side] = value.astype(sum1.dtype)
        third.start()
        for copy in after_copies:
            copy.wait_recv()
        value = sumz[row].astype(jnp.float32)
        for t in range(rows - 1):
            value = value + partb[t].astype(jnp.float32)
        share[quarter:] = value.astype(share.dtype)
        publish(1)
        third.wait_recv()
        value = sum1[side_of].astype(jnp.float32) + part2[...].astype(jnp.float32)
        share[:quarter] = value.astype(share.dtype)
        publish(0)
        start = pl.multiple_of(core * half + side_of * height, height)
        full[pl.ds(start, height), :] = share[...]
        landed(core, 1 - side_of, 0)
        relay(1 - side_of, 4).start()

    @pl.when(jnp.logical_not(owner))
    def _():
        landed(core, side_of, 0)
        relay(side_of, 4).start()
        landed(core, 1 - side_of, 0)
        relay(1 - side_of, 5).start()

    window.wait()
    result = jnp.dot(
        window_ref[:, mine_half], full[mine_half, :], preferred_element_type=jnp.float32
    )
    for side in range(OWNERS):
        landed(1 - core, side, 1)
    out_ref[...] = result + jnp.dot(
        window_ref[:, other_half], full[other_half, :], preferred_element_type=jnp.float32
    )

    @pl.when(owner)
    def _():
        for copy in sum(second_copies, first_copies + across_copies + after_copies):
            copy.wait_send()
        for copy in [third] + last_copies:
            copy.wait_send()
        relay(1 - side_of, 4).wait_send()

    @pl.when(jnp.logical_not(owner))
    def _():
        relay(side_of, 4).wait_send()
        relay(1 - side_of, 5).wait_send()

    direct.wait_send()
    for route in range(len(routes)):
        d = routes[route][0]
        came, valid = origin(route)
        for h in range(SPLIT):
            there, sent = towards(route, h)
            special = d == 1 and h == SPLIT - 1

            @pl.when(sent)
            def _():
                z_copy(route, h, (row, there * CORES + core)).wait_send()

            @pl.when(valid & (came != mate) if special else valid)
            def _():
                for t in range(1, rows):
                    spread(row, came, h, t, row_peers[rows - t - 1]).wait_send()

    for came in range(chips):
        for h in range(SPLIT):

            @pl.when(owner)
            def _():
                for k in range(1, owners):
                    handout(came, h, k).wait_send()

            @pl.when(jnp.logical_not(owner))
            def _():
                for side in range(OWNERS):
                    along(came, h, side).wait_send()
                for t in range(1, rows):
                    across(came, h, t).wait_send()
                    for side in range(OWNERS):
                        onwards(came, h, t, side).wait_send()


def exchange(integrals, ids, coefficients, metric, rows, orbs, blocks, count):
    chips = orbs // CORES
    orb_local, basis = coefficients.shape
    aux_local, local_rows, _ = integrals.shape
    tile = local_rows // blocks
    owners = rows * OWNERS
    piece = orb_local // rows // SPLIT
    group = piece * rows
    part = group // owners
    aux = aux_local * orbs
    window = local_rows * rows
    half = window // CORES
    height = half // OWNERS
    quarter = height // 2
    routes = 2 * (chips - 1)
    dtype = coefficients.dtype
    scratch = [
        pltpu.VMEM((basis // tile, piece, tile), dtype) for _ in range(routes * SPLIT)
    ]
    scratch += [
        pltpu.VMEM((basis // tile, orb_local, tile), dtype),
        pltpu.VMEM((chips, SPLIT, group, count * tile), dtype),
        pltpu.VMEM((chips - 1, SPLIT, rows - 1, piece, count * tile), dtype),
        pltpu.VMEM((CORES,) + integrals.shape, dtype),
        pltpu.VMEM((chips, SPLIT, owners, CORES * aux_local, part, local_rows), dtype),
        pltpu.VMEM((rows, 1, ids.shape[1]), jnp.int32),
        pltpu.SMEM((rows, 1, ids.shape[1]), jnp.int32),
        pltpu.VMEM((chips, SPLIT, rows, chips, CORES * aux_local, part, local_rows), dtype),
        pltpu.VMEM((2, aux * part, aux * part), dtype),
        pltpu.VMEM((window, aux * part), dtype),
        pltpu.VMEM((rows, aux * part, local_rows), dtype),
        pltpu.VMEM((rows, window, local_rows), jnp.float32),
        pltpu.VMEM((rows, half, local_rows), dtype),
        pltpu.VMEM((rows, half, local_rows), dtype),
        pltpu.VMEM((rows, half, local_rows), dtype),
        pltpu.VMEM((rows - 1, OWNERS, quarter, local_rows), dtype),
        pltpu.VMEM((OWNERS, quarter, local_rows), dtype),
        pltpu.VMEM((quarter, local_rows), dtype),
        pltpu.VMEM((height, local_rows), dtype),
        pltpu.VMEM((window, local_rows), dtype),
        pltpu.VMEM((orb_local, window), dtype),
        pltpu.SemaphoreType.DMA((routes, SPLIT)),
        pltpu.SemaphoreType.DMA((routes, SPLIT)),
        pltpu.SemaphoreType.DMA((chips - 1, SPLIT, rows)),
        pltpu.SemaphoreType.DMA((chips - 1, SPLIT, rows)),
        pltpu.SemaphoreType.DMA((5 + SPLIT,)),
        pltpu.SemaphoreType.DMA((rows,)),
        pltpu.SemaphoreType.DMA((rows,)),
        pltpu.SemaphoreType.DMA((chips, SPLIT, owners)),
        pltpu.SemaphoreType.DMA((chips, SPLIT, rows * chips)),
        pltpu.SemaphoreType.DMA,
        pltpu.SemaphoreType.DMA,
        pltpu.VMEM(
            (chips, SPLIT, rows - 1, OWNERS, CORES * aux_local, part, local_rows), dtype
        ),
        pltpu.SemaphoreType.DMA((chips, SPLIT, rows - 1)),
        pltpu.SemaphoreType.DMA((chips, SPLIT, rows - 1, OWNERS)),
        pltpu.SemaphoreType.DMA((rows,)),
        pltpu.SemaphoreType.DMA((rows,)),
        pltpu.SemaphoreType.DMA((rows, OWNERS)),
        pltpu.SemaphoreType.DMA((rows, OWNERS)),
        pltpu.SemaphoreType.DMA,
        pltpu.SemaphoreType.DMA,
        pltpu.SemaphoreType.DMA((6,)),
        pltpu.SemaphoreType.DMA((2, OWNERS)),
        pltpu.VMEM((rows, quarter, local_rows), dtype),
        pltpu.VMEM((rows, quarter, local_rows), dtype),
        pltpu.VMEM((rows - 1, quarter, local_rows), dtype),
        pltpu.SemaphoreType.DMA((rows,)),
        pltpu.SemaphoreType.DMA((rows,)),
        pltpu.SemaphoreType.DMA((rows,)),
        pltpu.SemaphoreType.DMA((rows,)),
        pltpu.VMEM((SPLIT, basis // tile, piece, tile), dtype),
    ]
    dims = (rows, chips, orb_local, tile, count, aux_local, blocks, part)
    return pl.pallas_call(
        functools.partial(exchange_kernel, dims),
        out_shape=jax.ShapeDtypeStruct((orb_local, local_rows), jnp.float32),
        in_specs=[pl.BlockSpec(memory_space=pltpu.VMEM)] * 2
        + [pl.BlockSpec(memory_space=pl.ANY)] * 2,
        out_specs=pl.BlockSpec(memory_space=pltpu.VMEM),
        scratch_shapes=scratch,
        compiler_params=pltpu.CompilerParams(
            collective_id=0, has_side_effects=True, vmem_limit_bytes=63 << 20
        ),
    )(ids, metric, coefficients, integrals)


def per_device(rows, orbs, integrals, tile_ids, coefficients, metric):
    orb_local, basis_width = coefficients.shape
    block_count, kept_count = tile_ids.shape
    chips = orbs // CORES
    if (
        chips != 2 * OWNERS
        or orb_local % (16 * SPLIT * rows)
        or orb_local % (8 * SPLIT * OWNERS * rows)
        or block_count * kept_count % 8
        or basis_width // (integrals.shape[1] // block_count) % 8
    ):
        return plain_device(rows, orbs, integrals, tile_ids, coefficients, metric)
    count = block_count * kept_count
    lanes = -(-count // 128) * 128
    ids = jnp.pad(tile_ids.reshape(1, count), ((0, 0), (0, lanes - count)))
    return exchange(integrals, ids, coefficients, metric, rows, orbs, block_count, count)


def plain_device(rows, orbs, integrals, tile_ids, coefficients, metric):
    aux_local, local_rows, kept_width = integrals.shape
    orb_local, basis_width = coefficients.shape
    block_count, kept_count = tile_ids.shape
    tile_rows = local_rows // block_count
    orbitals = orb_local * orbs
    aux = aux_local * orbs
    window = local_rows * rows
    part = orbitals // (rows * orbs)
    picked = pick(coefficients, tile_ids.reshape(block_count * kept_count), tile_rows)
    col_piece = lax.all_gather(picked, "orb", axis=0, tiled=True)
    slabs = integrals.reshape(aux_local, block_count, tile_rows, kept_width)
    halves = [
        jnp.einsum(
            "pmk,jk->pjm",
            slabs[:, b],
            col_piece[:, b * kept_width : (b + 1) * kept_width],
            preferred_element_type=jnp.float32,
        ).astype(jnp.bfloat16)
        for b in range(block_count)
    ]
    halves = jnp.concatenate(halves, axis=2)
    outgoing = halves.reshape(aux_local, rows * orbs, part, local_rows).transpose(1, 0, 2, 3)
    by_part = lax.all_to_all(outgoing, ("row", "orb"), split_axis=0, concat_axis=0, tiled=True)
    by_part = by_part.reshape(rows, aux, part, local_rows)
    mixed = jnp.einsum(
        "pq,rpjm->rqjm", metric, by_part.astype(jnp.float32), precision=lax.Precision.HIGHEST
    ).astype(jnp.bfloat16)
    gram = jnp.einsum(
        "rqjm,sqjn->rmsn", by_part, mixed, preferred_element_type=jnp.float32
    ).astype(jnp.bfloat16)
    gram = gram.reshape(orbs, window // orbs, rows, local_rows).transpose(2, 0, 1, 3)
    gram = gram.reshape(rows * window, local_rows)
    share = lax.psum_scatter(gram, ("row", "orb"), scatter_dimension=0, tiled=True)
    columns = lax.all_gather(share, "orb", axis=0, tiled=True)
    return jnp.dot(coefficients[:, :window], columns, preferred_element_type=jnp.float32)


def solution(mesh):
    return jax.shard_map(
        functools.partial(per_device, mesh.shape["row"], mesh.shape["orb"]),
        mesh=mesh,
        in_specs=(P("orb", "row", None), P("row", None), P("orb", None), P()),
        out_specs=P("orb", "row"),
        check_vma=False,
    )
```

```python
import functools

import jax
import jax.numpy as jnp
from jax import lax
from jax.experimental import pallas as pl
from jax.experimental.pallas import tpu as pltpu
from jax.sharding import PartitionSpec as P


def pick_kernel(count, tile, ids_ref, coef_ref, out_ref, sem):
    def begin(slot, carry):
        source = pl.ds(pl.multiple_of(ids_ref[slot] * tile, tile), tile)
        target = pl.ds(pl.multiple_of(slot * tile, tile), tile)
        pltpu.make_async_copy(coef_ref.at[:, source], out_ref.at[:, target], sem).start()
        return carry

    lax.fori_loop(0, count, begin, 0)
    pltpu.make_async_copy(coef_ref.at[:, pl.ds(0, count * tile)], out_ref, sem).wait()


def pick(coefficients, ids, tile):
    count = ids.shape[0]
    return pl.pallas_call(
        functools.partial(pick_kernel, count, tile),
        out_shape=jax.ShapeDtypeStruct((coefficients.shape[0], count * tile), coefficients.dtype),
        in_specs=[
            pl.BlockSpec(memory_space=pltpu.SMEM),
            pl.BlockSpec(memory_space=pl.ANY),
        ],
        out_specs=pl.BlockSpec(memory_space=pltpu.VMEM),
        scratch_shapes=[pltpu.SemaphoreType.DMA],
    )(ids, coefficients)


MESH = pl.DeviceIdType.MESH
CORES = 2
SPLIT = 2
OWNERS = 2


def greet(peers):
    barrier = pltpu.get_barrier_semaphore()
    for peer in peers:
        pl.semaphore_signal(barrier, inc=1, device_id=peer, device_id_type=MESH)
    pl.semaphore_wait(barrier, len(peers))


def remote(source, target, send, recv, device):
    return pltpu.make_async_remote_copy(
        src_ref=source,
        dst_ref=target,
        send_sem=send,
        recv_sem=recv,
        device_id=device,
        device_id_type=MESH,
    )


def exchange_kernel(dims, ids_ref, metric_ref, coef_ref, ints_ref, out_ref, *scratch):
    rows, chips, orb_local, tile, count, aux_local, blocks, part = dims
    piece = orb_local // rows // SPLIT
    group = piece * rows
    routes = [(d, s) for d in range(1, chips) for s in (1, -1)]
    scratch = list(scratch)
    raw = {}
    for route in range(len(routes)):
        for h in range(SPLIT):
            raw[route, h] = scratch.pop(0)
    own, kept, staged, both, ready, ids_v, ids_s = scratch[:7]
    first_rows = scratch.pop()
    partz, sumz, partb, sendz, recvz, sendb, recvb = scratch[-7:]
    scratch = scratch[:-7]
    parts, weight, crossed, mixed, total_ref = scratch[7:12]
    gram, part0, sum0, part1, sum1, part2, share, full, window_ref = scratch[12:21]
    z_send, z_recv, p_send, p_recv, l_sem, i_send, i_recv, x_send, x_recv = scratch[21:30]
    q_send, q_recv, relayed, y_recv, y_send = scratch[30:35]
    send0, recv0, send1, recv1, send2, recv2, send3, recv3 = scratch[35:]
    width = count * tile // blocks
    total = rows * chips
    owners = rows * OWNERS
    row = lax.axis_index("row")
    orb = lax.axis_index("orb")
    chip = orb // CORES
    core = orb % CORES
    row_peers = [(lax.rem(row + t, rows), orb) for t in range(1, rows)]
    partner = (row, chip * CORES + 1 - core)
    me = row * chips + chip
    side_of = chip // 2
    mate = chip + 1 - 2 * (chip % 2)
    owner = (chip > 0) & (chip < chips - 1)
    home = row * OWNERS + side_of

    def place(k):
        other = lax.rem(me + k, total)
        return (other // chips, lax.rem(other, chips) * CORES + core)

    greet([place(k) for k in range(1, total)] + [partner])

    window = pltpu.make_async_copy(
        coef_ref.at[:, pl.ds(0, window_ref.shape[1])], window_ref, l_sem.at[4]
    )

    def z_copy(route, h, device):
        return remote(
            first_rows.at[h] if routes[route][0] == 1 else raw[route - 2, h],
            raw[route, h],
            z_send.at[route, h],
            z_recv.at[route, h],
            device,
        )

    def inside(where):
        return (where >= 0) & (where < chips)

    def towards(route, h):
        d, s = routes[route]
        there = chip + s
        valid = inside(there) & inside(chip - s * (d - 1))
        if d == 1 and h == SPLIT - 1:
            valid = valid & inside(there + s)
        return there, valid

    def origin(route):
        d, s = routes[route]
        there = chip - s * d
        return there, inside(there)

    tiles = own.shape[0]

    def every(source_rows, target, sem, act):
        step = 8

        def some(index, carry):
            for n in range(step):
                which = index * step + n
                at = pl.ds(pl.multiple_of(which * tile, tile), tile)
                act(pltpu.make_async_copy(coef_ref.at[source_rows, at], target.at[which], sem))
            return carry

        lax.fori_loop(0, tiles // step, some, 0)

    def first_piece(h, act):
        start = pl.multiple_of(h * group + row * piece, piece)
        every(pl.ds(start, piece), first_rows.at[h], l_sem.at[5 + h], act)

    all_rows = pl.ds(0, orb_local)
    for h in range(SPLIT):
        first_piece(h, lambda copy: copy.start())
    bring = pltpu.make_async_copy(ints_ref, both.at[0], l_sem.at[2])
    swap = remote(ints_ref, both.at[1], i_send.at[0], i_recv.at[0], partner)
    for h in range(SPLIT):
        first_piece(h, lambda copy: copy.wait())
        for route in range(2):
            there, valid = towards(route, h)

            @pl.when(valid)
            def _():
                z_copy(route, h, (row, there * CORES + core)).start()

    every(all_rows, own, l_sem.at[0], lambda copy: copy.start())
    bring.start()
    swap.start()
    id_copies = []
    for t in range(1, rows):
        id_copies.append(
            remote(ids_ref, ids_v.at[t], i_send.at[t], i_recv.at[t], row_peers[t - 1])
        )
        id_copies[-1].start()

    window.start()
    first = pltpu.make_async_copy(ids_ref, ids_s.at[0], l_sem.at[1])
    first.start()
    first.wait()
    for t in range(1, rows):
        id_copies[t - 1].wait()
        move = pltpu.make_async_copy(ids_v.at[t], ids_s.at[t], l_sem.at[1])
        move.start()
        move.wait()

    def take(source, targets, t):
        step = 8

        def some(block, carry):
            for k in range(step):
                slot = block * step + k
                at = pl.ds(pl.multiple_of(slot * tile, tile), tile)
                value = source[ids_s[t, 0, slot]]
                height = value.shape[0] // len(targets)
                for n, target in enumerate(targets):
                    target[:, at] = value[n * height : (n + 1) * height]
            return carry

        lax.fori_loop(0, count // step, some, 0)

    def band(from_row):
        return pl.ds(pl.multiple_of(from_row * piece, piece), piece)

    def spread(from_row, came, h, t, device):
        k = lax.rem(came + chips - chip, chips) - 1
        return remote(
            staged.at[k, h, t - 1],
            kept.at[came, h, band(from_row), :],
            p_send.at[k, h, t],
            p_recv.at[k, h, t],
            device,
        )

    direct = remote(
        kept.at[chip, SPLIT - 1],
        kept.at[chip, SPLIT - 1],
        q_send,
        q_recv,
        (row, mate * CORES + core),
    )

    whole = pl.ds(0, CORES * aux_local)

    def handout(came, h, k, some=whole):
        to = lax.rem(home + k, owners)
        return remote(
            ready.at[came, h, to, some],
            parts.at[came, h, row, chip, some],
            x_send.at[came, h, k],
            x_recv.at[came, h, me],
            (to // OWNERS, (1 + lax.rem(to, OWNERS)) * CORES + core),
        )

    def keep(came, h, some=whole):
        return pltpu.make_async_copy(
            ready.at[came, h, home, some],
            parts.at[came, h, row, chip, some],
            x_send.at[came, h, 0],
        )

    def along(came, h, side, some=whole):
        return remote(
            ready.at[came, h, row * OWNERS + side, some],
            parts.at[came, h, row, chip, some],
            x_send.at[came, h, side],
            x_recv.at[came, h, me],
            (row, (1 + side) * CORES + core),
        )

    def across(came, h, t, some=whole):
        to = lax.rem(row + t, rows)
        return remote(
            ready.at[came, h, pl.ds(to * OWNERS, OWNERS), some],
            relayed.at[came, h, t - 1, :, some],
            x_send.at[came, h, OWNERS + t],
            y_recv.at[came, h, t - 1],
            (to, orb),
        )

    def onwards(came, h, t, side):
        source = lax.rem(row + rows - t, rows)
        return remote(
            relayed.at[came, h, t - 1, side],
            parts.at[came, h, source, chip],
            y_send.at[came, h, t - 1, side],
            x_recv.at[came, h, source * chips + chip],
            (row, (1 + side) * CORES + core),
        )

    def hand(came, h, some=whole):
        @pl.when(owner)
        def _():
            keep(came, h, some).start()
            for k in range(1, owners):
                handout(came, h, k, some).start()

        @pl.when(jnp.logical_not(owner))
        def _():
            for t in range(1, rows):
                across(came, h, t, some).start()
            for side in range(OWNERS):
                along(came, h, side, some).start()

    def forward(came, h):
        for t in range(1, rows):
            across(came, h, t).wait_recv()
            for side in range(OWNERS):
                onwards(came, h, t, side).start()

    def slot_of(side):
        return (core + side - 2 * core * side) * aux_local

    def some_products(lhs_of, side, block, store):
        lhs = lhs_of(pl.ds(pl.multiple_of(block * width, width), width))
        at = pl.ds(pl.multiple_of(block * tile, tile), tile)
        rhs = both[side, :, at, :].reshape(aux_local * tile, width)
        result = lax.dot_general(
            lhs, rhs, (((1,), (1,)), ((), ())), preferred_element_type=jnp.float32
        )
        for p in range(aux_local):
            value = result[:, p * tile : (p + 1) * tile].astype(ready.dtype)
            store(slot_of(side) + p, at, value)

    def product(came, h):
        def one(step, carry):
            side = step // blocks

            def store(slot, at, value):
                ready[came, h, :, slot, :, at] = value.reshape(owners, part, tile)

            some_products(
                lambda at: kept[came, h, :, at], side, step - side * blocks, store
            )
            return carry

        lax.fori_loop(0, CORES * blocks, one, 0)

        hand(came, h)

    def own_product(side):
        def one(block, carry):
            def store(slot, at, value):
                for h in range(SPLIT):
                    rows_of_h = value[h * group : (h + 1) * group]
                    ready[chip, h, :, slot, :, at] = rows_of_h.reshape(owners, part, tile)

            some_products(
                lambda at: kept[chip, :, :, at].reshape(orb_local, width), side, block, store
            )
            return carry

        lax.fori_loop(0, blocks, one, 0)
        some = pl.ds(slot_of(side), aux_local)
        for h in range(SPLIT):
            hand(chip, h, some)

    every(all_rows, own, l_sem.at[0], lambda copy: copy.wait())
    take(own, [kept.at[chip, h] for h in range(SPLIT)], 0)

    @pl.when(jnp.logical_not(owner))
    def _():
        direct.start()

    def pass_on(d):
        for h in range(SPLIT):
            for route in range(len(routes)):
                if routes[route][0] != d:
                    continue
                s = routes[route][1]
                came, valid = origin(route)
                special = d == 1 and h == SPLIT - 1

                @pl.when(valid & inside(chip + s) if special else valid)
                def _():
                    z_copy(route, h, partner).wait_recv()
                    if d + 1 < chips:
                        there, onward = towards(route + 2, h)

                        @pl.when(onward)
                        def _():
                            z_copy(route + 2, h, (row, there * CORES + core)).start()

                @pl.when(valid & (came != mate) if special else valid)
                def _():
                    k = lax.rem(came + chips - chip, chips) - 1
                    for t in range(1, rows):
                        take(raw[route, h], [staged.at[k, h, t - 1]], t)
                        spread(row, came, h, t, row_peers[rows - t - 1]).start()
                    take(raw[route, h], [kept.at[came, h, band(row), :]], 0)

    def multiply(d, pieces=range(SPLIT)):
        for h in pieces:
            for route in range(len(routes)):
                if routes[route][0] != d:
                    continue
                came, valid = origin(route)
                special = d == 1 and h == SPLIT - 1

                @pl.when(valid & (came != mate) if special else valid)
                def _():
                    for t in range(1, rows):
                        source_row = lax.rem(row + t, rows)
                        spread(source_row, came, h, t, row_peers[0]).wait_recv()
                    product(came, h)

    def multiply_direct():
        remote(
            kept.at[mate, SPLIT - 1], kept.at[mate, SPLIT - 1], q_send, q_recv, partner
        ).wait_recv()
        product(mate, SPLIT - 1)

    def prepare():
        height = weight.shape[1]
        aux = metric_ref.shape[0]
        at = lax.broadcasted_iota(jnp.int32, (height, aux), 0)
        which = lax.broadcasted_iota(jnp.int32, (height, aux), 1)
        expand = jnp.where(at // part == which, 1.0, 0.0).astype(jnp.float32)
        left = lax.dot_general(
            expand,
            metric_ref[...],
            (((1,), (1,)), ((), ())),
            precision=lax.Precision.HIGHEST,
            preferred_element_type=jnp.float32,
        )
        wide = lax.dot_general(
            left,
            expand,
            (((1,), (1,)), ((), ())),
            precision=lax.Precision.HIGHEST,
            preferred_element_type=jnp.float32,
        )
        a = lax.broadcasted_iota(jnp.int32, (height, height), 0)
        b = lax.broadcasted_iota(jnp.int32, (height, height), 1)
        wide = jnp.where(a % part == b % part, wide, 0.0)
        high = wide.astype(weight.dtype)
        weight[0] = high
        weight[1] = (wide - high.astype(jnp.float32)).astype(weight.dtype)
        for r in range(rows):
            total_ref[r] = jnp.zeros(total_ref.shape[1:], jnp.float32)

    bring.wait()
    own_product(0)
    pass_on(1)
    swap.wait()
    own_product(1)
    pass_on(2)

    @pl.when(owner)
    def _():
        direct.start()
        prepare()

    end = jnp.logical_not(owner)
    inward = 1 - 2 * side_of

    @pl.when(end)
    def _():
        for h in range(SPLIT):
            forward(chip, h)

    multiply(1)

    @pl.when(owner)
    def _():
        multiply_direct()

    @pl.when(end)
    def _():
        forward(mate, 0)

    pass_on(3)

    multiply(2)
    multiply(3, [0])

    @pl.when(end)
    def _():
        for h in range(SPLIT):
            forward(chip + 2 * inward, h)
        multiply_direct()
        forward(chip + 3 * inward, 0)

    multiply(3, [1])

    @pl.when(end)
    def _():
        forward(mate, SPLIT - 1)
        forward(chip + 3 * inward, SPLIT - 1)

    def collect(came, h):
        def arrive(k, carry):
            source = lax.rem(me + k, total)
            remote(
                ready.at[came, h, 0],
                parts.at[came, h, source // chips, lax.rem(source, chips)],
                x_send.at[came, h, 0],
                x_recv.at[came, h, source],
                partner,
            ).wait_recv()
            return carry

        lax.fori_loop(1, total, arrive, 0)
        keep(came, h).wait()
        height = weight.shape[1]
        local = mixed.shape[2]
        for r in range(rows):
            value = parts[came, h, r].astype(jnp.float32).reshape(height, local)
            value = value.astype(mixed.dtype)
            result = jnp.dot(weight[0], value, preferred_element_type=jnp.float32)
            result = result + jnp.dot(weight[1], value, preferred_element_type=jnp.float32)
            mixed[r] = result.astype(mixed.dtype)
            crossed[r * local : (r + 1) * local, :] = value.T

        def add(r, carry):
            total_ref[r] += jnp.dot(
                crossed[...], mixed[r], preferred_element_type=jnp.float32
            )
            return carry

        lax.fori_loop(0, rows, add, 0)

    height = share.shape[0]
    half = height * OWNERS
    quarter = height // 2
    first_copies, second_copies, last_copies = [], [], []
    across_copies, after_copies = [], []
    order = [lax.rem(row + t, rows) for t in range(1, rows)] + [row]
    near = 1 + side_of
    far = OWNERS - side_of
    for t, peer in enumerate(order):
        first_copies.append(
            remote(gram.at[peer], part0.at[peer], send0.at[t], recv0.at[t], partner)
        )
        start = pl.multiple_of((1 - side_of) * height + quarter, quarter)
        across_copies.append(
            remote(
                sum0.at[peer, pl.ds(start, quarter)],
                partz.at[peer],
                sendz.at[t],
                recvz.at[t],
                (row, far * CORES + core),
            )
        )
        if t < rows - 1:
            second_copies.append(
                [
                    remote(
                        sum0.at[peer, pl.ds(side * height, quarter)],
                        part1.at[t, side],
                        send1.at[t, side],
                        recv1.at[t, side],
                        (peer, orb),
                    )
                    for side in range(OWNERS)
                ]
            )
            after_copies.append(
                remote(sumz.at[peer], partb.at[t], sendb.at[t], recvb.at[t], (peer, orb))
            )
    third = remote(
        sum1.at[1 - side_of], part2, send2, recv2, (row, far * CORES + core)
    )

    def block(from_core, from_side):
        start = pl.multiple_of(from_core * half + from_side * height, height)
        return full.at[pl.ds(start, height), :]

    own_block = block(core, side_of)
    targets = [
        ((row, far * CORES + core), 0),
        ((row, mate * CORES + core), 0),
        ((row, (chips - 1 - mate) * CORES + core), 0),
        (partner, 1),
    ]
    for n, (device, kind) in enumerate(targets):
        last_copies.append(
            remote(share, own_block, send3.at[n], recv3.at[kind, side_of], device)
        )

    def publish(which):
        at = which * quarter
        start = core * half + side_of * height + at
        target = full.at[pl.ds(pl.multiple_of(start, quarter), quarter), :]
        for n, (device, kind) in enumerate(targets):
            remote(
                share.at[pl.ds(at, quarter)],
                target,
                send3.at[n],
                recv3.at[kind, side_of],
                device,
            ).start()

    def relay(side, n):
        return remote(
            block(core, side), block(core, side), send3.at[n], recv3.at[1, side], partner
        )

    def landed(from_core, side, kind):
        remote(
            share, block(from_core, side), send3.at[0], recv3.at[kind, side], partner
        ).wait_recv()

    mine_half = pl.ds(pl.multiple_of(core * half, half), half)
    other_half = pl.ds(pl.multiple_of((1 - core) * half, half), half)

    @pl.when(owner)
    def _():
        def inner(u, carry):
            collect(1 + lax.rem(u, 2), u // 2)
            return carry

        def outer(u, carry):
            collect((chips - 1) * lax.rem(u, 2), u // 2)
            return carry

        for h in range(SPLIT):
            lax.fori_loop(h * OWNERS, (h + 1) * OWNERS, inner, 0)
            lax.fori_loop(h * OWNERS, (h + 1) * OWNERS, outer, 0)
        for t, peer in enumerate(order):
            gram[peer] = total_ref[peer, other_half].astype(gram.dtype)
            first_copies[t].start()
        for t, peer in enumerate(order):
            first_copies[t].wait_recv()
            value = total_ref[peer, mine_half] + part0[peer].astype(jnp.float32)
            sum0[peer] = value.astype(sum0.dtype)
            across_copies[t].start()
            if t < rows - 1:
                for copy in second_copies[t]:
                    copy.start()
        for t, peer in enumerate(order):
            across_copies[t].wait_recv()
            start = pl.multiple_of(side_of * height + quarter, quarter)
            value = sum0[peer, pl.ds(start, quarter)].astype(jnp.float32)
            sumz[peer] = (value + partz[peer].astype(jnp.float32)).astype(sumz.dtype)
            if t < rows - 1:
                after_copies[t].start()
        for copies in second_copies:
            for copy in copies:
                copy.wait_recv()
        for side in range(OWNERS):
            value = sum0[row, side * height : side * height + quarter].astype(jnp.float32)
            for t in range(rows - 1):
                value = value + part1[t, side].astype(jnp.float32)
            sum1[side] = value.astype(sum1.dtype)
        third.start()
        for copy in after_copies:
            copy.wait_recv()
        value = sumz[row].astype(jnp.float32)
        for t in range(rows - 1):
            value = value + partb[t].astype(jnp.float32)
        share[quarter:] = value.astype(share.dtype)
        publish(1)
        third.wait_recv()
        value = sum1[side_of].astype(jnp.float32) + part2[...].astype(jnp.float32)
        share[:quarter] = value.astype(share.dtype)
        publish(0)
        start = pl.multiple_of(core * half + side_of * height, height)
        full[pl.ds(start, height), :] = share[...]
        landed(core, 1 - side_of, 0)
        relay(1 - side_of, 4).start()

    @pl.when(jnp.logical_not(owner))
    def _():
        landed(core, side_of, 0)
        relay(side_of, 4).start()
        landed(core, 1 - side_of, 0)
        relay(1 - side_of, 5).start()

    window.wait()
    result = jnp.dot(
        window_ref[:, mine_half], full[mine_half, :], preferred_element_type=jnp.float32
    )
    for side in range(OWNERS):
        landed(1 - core, side, 1)
    out_ref[...] = result + jnp.dot(
        window_ref[:, other_half], full[other_half, :], preferred_element_type=jnp.float32
    )

    @pl.when(owner)
    def _():
        for copy in sum(second_copies, first_copies + across_copies + after_copies):
            copy.wait_send()
        for copy in [third] + last_copies:
            copy.wait_send()
        relay(1 - side_of, 4).wait_send()

    @pl.when(jnp.logical_not(owner))
    def _():
        relay(side_of, 4).wait_send()
        relay(1 - side_of, 5).wait_send()

    direct.wait_send()
    for route in range(len(routes)):
        d = routes[route][0]
        came, valid = origin(route)
        for h in range(SPLIT):
            there, sent = towards(route, h)
            special = d == 1 and h == SPLIT - 1

            @pl.when(sent)
            def _():
                z_copy(route, h, (row, there * CORES + core)).wait_send()

            @pl.when(valid & (came != mate) if special else valid)
            def _():
                for t in range(1, rows):
                    spread(row, came, h, t, row_peers[rows - t - 1]).wait_send()

    for came in range(chips):
        for h in range(SPLIT):

            @pl.when(owner)
            def _():
                for k in range(1, owners):
                    handout(came, h, k).wait_send()

            @pl.when(jnp.logical_not(owner))
            def _():
                for side in range(OWNERS):
                    along(came, h, side).wait_send()
                for t in range(1, rows):
                    across(came, h, t).wait_send()
                    for side in range(OWNERS):
                        onwards(came, h, t, side).wait_send()


def exchange(integrals, ids, coefficients, metric, rows, orbs, blocks, count):
    chips = orbs // CORES
    orb_local, basis = coefficients.shape
    aux_local, local_rows, _ = integrals.shape
    tile = local_rows // blocks
    owners = rows * OWNERS
    piece = orb_local // rows // SPLIT
    group = piece * rows
    part = group // owners
    aux = aux_local * orbs
    window = local_rows * rows
    half = window // CORES
    height = half // OWNERS
    quarter = height // 2
    routes = 2 * (chips - 1)
    dtype = coefficients.dtype
    scratch = [
        pltpu.VMEM((basis // tile, piece, tile), dtype) for _ in range(routes * SPLIT)
    ]
    scratch += [
        pltpu.VMEM((basis // tile, orb_local, tile), dtype),
        pltpu.VMEM((chips, SPLIT, group, count * tile), dtype),
        pltpu.VMEM((chips - 1, SPLIT, rows - 1, piece, count * tile), dtype),
        pltpu.VMEM((CORES,) + integrals.shape, dtype),
        pltpu.VMEM((chips, SPLIT, owners, CORES * aux_local, part, local_rows), dtype),
        pltpu.VMEM((rows, 1, ids.shape[1]), jnp.int32),
        pltpu.SMEM((rows, 1, ids.shape[1]), jnp.int32),
        pltpu.VMEM((chips, SPLIT, rows, chips, CORES * aux_local, part, local_rows), dtype),
        pltpu.VMEM((2, aux * part, aux * part), dtype),
        pltpu.VMEM((window, aux * part), dtype),
        pltpu.VMEM((rows, aux * part, local_rows), dtype),
        pltpu.VMEM((rows, window, local_rows), jnp.float32),
        pltpu.VMEM((rows, half, local_rows), dtype),
        pltpu.VMEM((rows, half, local_rows), dtype),
        pltpu.VMEM((rows, half, local_rows), dtype),
        pltpu.VMEM((rows - 1, OWNERS, quarter, local_rows), dtype),
        pltpu.VMEM((OWNERS, quarter, local_rows), dtype),
        pltpu.VMEM((quarter, local_rows), dtype),
        pltpu.VMEM((height, local_rows), dtype),
        pltpu.VMEM((window, local_rows), dtype),
        pltpu.VMEM((orb_local, window), dtype),
        pltpu.SemaphoreType.DMA((routes, SPLIT)),
        pltpu.SemaphoreType.DMA((routes, SPLIT)),
        pltpu.SemaphoreType.DMA((chips - 1, SPLIT, rows)),
        pltpu.SemaphoreType.DMA((chips - 1, SPLIT, rows)),
        pltpu.SemaphoreType.DMA((5 + SPLIT,)),
        pltpu.SemaphoreType.DMA((rows,)),
        pltpu.SemaphoreType.DMA((rows,)),
        pltpu.SemaphoreType.DMA((chips, SPLIT, owners)),
        pltpu.SemaphoreType.DMA((chips, SPLIT, rows * chips)),
        pltpu.SemaphoreType.DMA,
        pltpu.SemaphoreType.DMA,
        pltpu.VMEM(
            (chips, SPLIT, rows - 1, OWNERS, CORES * aux_local, part, local_rows), dtype
        ),
        pltpu.SemaphoreType.DMA((chips, SPLIT, rows - 1)),
        pltpu.SemaphoreType.DMA((chips, SPLIT, rows - 1, OWNERS)),
        pltpu.SemaphoreType.DMA((rows,)),
        pltpu.SemaphoreType.DMA((rows,)),
        pltpu.SemaphoreType.DMA((rows, OWNERS)),
        pltpu.SemaphoreType.DMA((rows, OWNERS)),
        pltpu.SemaphoreType.DMA,
        pltpu.SemaphoreType.DMA,
        pltpu.SemaphoreType.DMA((6,)),
        pltpu.SemaphoreType.DMA((2, OWNERS)),
        pltpu.VMEM((rows, quarter, local_rows), dtype),
        pltpu.VMEM((rows, quarter, local_rows), dtype),
        pltpu.VMEM((rows - 1, quarter, local_rows), dtype),
        pltpu.SemaphoreType.DMA((rows,)),
        pltpu.SemaphoreType.DMA((rows,)),
        pltpu.SemaphoreType.DMA((rows,)),
        pltpu.SemaphoreType.DMA((rows,)),
        pltpu.VMEM((SPLIT, basis // tile, piece, tile), dtype),
    ]
    dims = (rows, chips, orb_local, tile, count, aux_local, blocks, part)
    return pl.pallas_call(
        functools.partial(exchange_kernel, dims),
        out_shape=jax.ShapeDtypeStruct((orb_local, local_rows), jnp.float32),
        in_specs=[pl.BlockSpec(memory_space=pltpu.VMEM)] * 2
        + [pl.BlockSpec(memory_space=pl.ANY)] * 2,
        out_specs=pl.BlockSpec(memory_space=pltpu.VMEM),
        scratch_shapes=scratch,
        compiler_params=pltpu.CompilerParams(
            collective_id=0, has_side_effects=True, vmem_limit_bytes=63 << 20
        ),
    )(ids, metric, coefficients, integrals)


def per_device(rows, orbs, integrals, tile_ids, coefficients, metric):
    orb_local, basis_width = coefficients.shape
    block_count, kept_count = tile_ids.shape
    chips = orbs // CORES
    if (
        chips != 2 * OWNERS
        or orb_local % (16 * SPLIT * rows)
        or orb_local % (8 * SPLIT * OWNERS * rows)
        or block_count * kept_count % 8
        or basis_width // (integrals.shape[1] // block_count) % 8
    ):
        return plain_device(rows, orbs, integrals, tile_ids, coefficients, metric)
    count = block_count * kept_count
    lanes = -(-count // 128) * 128
    ids = jnp.pad(tile_ids.reshape(1, count), ((0, 0), (0, lanes - count)))
    return exchange(integrals, ids, coefficients, metric, rows, orbs, block_count, count)


def plain_device(rows, orbs, integrals, tile_ids, coefficients, metric):
    aux_local, local_rows, kept_width = integrals.shape
    orb_local, basis_width = coefficients.shape
    block_count, kept_count = tile_ids.shape
    tile_rows = local_rows // block_count
    orbitals = orb_local * orbs
    aux = aux_local * orbs
    window = local_rows * rows
    part = orbitals // (rows * orbs)
    picked = pick(coefficients, tile_ids.reshape(block_count * kept_count), tile_rows)
    col_piece = lax.all_gather(picked, "orb", axis=0, tiled=True)
    slabs = integrals.reshape(aux_local, block_count, tile_rows, kept_width)
    halves = [
        jnp.einsum(
            "pmk,jk->pjm",
            slabs[:, b],
            col_piece[:, b * kept_width : (b + 1) * kept_width],
            preferred_element_type=jnp.float32,
        ).astype(jnp.bfloat16)
        for b in range(block_count)
    ]
    halves = jnp.concatenate(halves, axis=2)
    outgoing = halves.reshape(aux_local, rows * orbs, part, local_rows).transpose(1, 0, 2, 3)
    by_part = lax.all_to_all(outgoing, ("row", "orb"), split_axis=0, concat_axis=0, tiled=True)
    by_part = by_part.reshape(rows, aux, part, local_rows)
    mixed = jnp.einsum(
        "pq,rpjm->rqjm", metric, by_part.astype(jnp.float32), precision=lax.Precision.HIGHEST
    ).astype(jnp.bfloat16)
    gram = jnp.einsum(
        "rqjm,sqjn->rmsn", by_part, mixed, preferred_element_type=jnp.float32
    ).astype(jnp.bfloat16)
    gram = gram.reshape(orbs, window // orbs, rows, local_rows).transpose(2, 0, 1, 3)
    gram = gram.reshape(rows * window, local_rows)
    share = lax.psum_scatter(gram, ("row", "orb"), scatter_dimension=0, tiled=True)
    columns = lax.all_gather(share, "orb", axis=0, tiled=True)
    return jnp.dot(coefficients[:, :window], columns, preferred_element_type=jnp.float32)


def solution(mesh):
    return jax.shard_map(
        functools.partial(per_device, mesh.shape["row"], mesh.shape["orb"]),
        mesh=mesh,
        in_specs=(P("orb", "row", None), P("row", None), P("orb", None), P()),
        out_specs=P("orb", "row"),
        check_vma=False,
    )
```
